32 devices in a mesh: seq: 8 (over z, y), tensor: 4 (over x, core).
Axes of the slice: x: 2, y: 2, z: 4, core: 2. Of those that a mesh axis runs over, the one named last changes fastest.
Arguments:
- block_input: bfloat16 [8192, 1024], P('seq', 'tensor'), may hold values from -8 to 8
- cotangent: bfloat16 [8192, 1024], P('seq', 'tensor'), may hold values from -6 to 6
- image_ids: int32 [8192], replicated, may hold values from -1 to 4, as said below
- qkv_weight: bfloat16 [1024, 3072], P('tensor', 'seq'), may hold values from -7 to 7
- proj_weight: bfloat16 [1024, 1024], P('tensor', 'seq'), may hold values from -1.5 to 1.5
- fc1_weight: bfloat16 [4096, 1024], P('tensor', 'seq'), may hold values from -0.1875 to 0.1875
- fc2_weight: bfloat16 [4096, 1024], P('tensor', 'seq'), may hold values from -0.09375 to 0.09375
- norm1_gain: float32 [1024], P('tensor'), may hold values from 0.25 to 1.75
- norm1_shift: float32 [1024], P('tensor'), may hold values from -3 to 3
- q_bias: float32 [1024], P('tensor'), may hold values from -3 to 3
- v_bias: float32 [1024], P('tensor'), may hold values from -3 to 3
- proj_bias: float32 [1024], P('tensor'), may hold values from -3 to 3
- scale_attn: float32 [1024], P('tensor'), may hold values from 0.5 to 2
- norm2_gain: float32 [1024], P('tensor'), may hold values from 0.25 to 1.75
- norm2_shift: float32 [1024], P('tensor'), may hold values from -3 to 3
- fc1_bias: float32 [4096], P('tensor'), may hold values from -3 to 3
- fc2_bias: float32 [1024], P('tensor'), may hold values from -3 to 3
- scale_mlp: float32 [1024], P('tensor'), may hold values from 0.5 to 2
Outputs:
- block_output: bfloat16 [8192, 1024], P('seq', 'tensor')
- input_grad: bfloat16 [8192, 1024], P('seq', 'tensor')
- qkv_weight_grad: float32 [1024, 3072], P('tensor', 'seq')
- proj_weight_grad: float32 [1024, 1024], P('tensor', 'seq')
- fc1_weight_grad: float32 [4096, 1024], P('tensor', 'seq')
- fc2_weight_grad: float32 [4096, 1024], P('tensor', 'seq')
- norm1_gain_grad: float32 [1024], P('tensor')
- norm1_shift_grad: float32 [1024], P('tensor')
- q_bias_grad: float32 [1024], P('tensor')
- v_bias_grad: float32 [1024], P('tensor')
- proj_bias_grad: float32 [1024], P('tensor')
- scale_attn_grad: float32 [1024], P('tensor')
- norm2_gain_grad: float32 [1024], P('tensor')
- norm2_shift_grad: float32 [1024], P('tensor')
- fc1_bias_grad: float32 [4096], P('tensor')
- fc2_bias_grad: float32 [1024], P('tensor')
- scale_mlp_grad: float32 [1024], P('tensor')
The draws below stay inside these ranges and needn't reach their ends.
Inputs may be any that keep to these rules, and one draw needn't show every extreme that they name: `image_ids`: tokens of one image are consecutive; there are exactly (5) images, numbered 0, 1, 2 in order of position; each has 686 to 1370 tokens and image 0 has exactly 1370; the tokens after the last image, at least one, are padding with id -1.
All inputs are finite; a program needn't handle non-finite values.
Results may differ from the reference program's by a relative error of at most 0.0095.
The reference program's roundings to bfloat16 on the way count: a program that leaves them out, or rounds other values in their place, can miss the bound.
Values may be sent and summed in bfloat16 or wider, within the bound.
No kernel may reach another device: no remote copies, remote signals or barrier semaphores. Data moves between devices by JAX's collectives and lax.ppermute only.
A program may use at most 256 MiB of HBM per device.

```python
import math
import jax
import jax.numpy as jnp
from jax import lax

D = 1024
HEADS = 16
HEAD_DIM = 64
FF = 4096
IMG = 1370
TOK_DEV = 1024
TOKENS = 8192
REACH = 2
N_SEQ = 8


def draw_block_input(key, part):
    base = jax.random.normal(key, (TOKENS, D), jnp.float32)
    return jnp.clip(base, -8.0, 8.0).astype(jnp.bfloat16)


def draw_qkv_weight(key, part):
    base = jax.random.normal(key, (D, 3 * D), jnp.float32) / math.sqrt(D)
    return jnp.clip(base, -7.0, 7.0).astype(jnp.bfloat16)


def draw_image_ids(key, part):
    number = (TOKENS - 1) // IMG
    lengths = jax.random.randint(key, (number,), IMG // 2 + 1, IMG + 1)
    lengths = jnp.where(jnp.arange(number) == 0, IMG, lengths).astype(jnp.int32)
    ends = jnp.cumsum(lengths)
    places = jnp.arange(TOKENS, dtype=jnp.int32)
    position = jnp.sum((ends[None, :] <= places[:, None]).astype(jnp.int32), axis=1)
    return jnp.where(position < number, position, -1).astype(jnp.int32)


def block_scale(rng, shape, split, least, top_value):
    level, own = 1.0, jax.random.fold_in(rng, 6)
    for dim, parts in split:
        draws = jnp.exp(jax.random.uniform(jax.random.fold_in(own, dim), (parts,), jnp.float32, least / len(split), top_value / len(split)))
        level = level * jnp.repeat(draws, shape[dim] // parts).reshape([-1 if axis == dim else 1 for axis in range(len(shape))])
    return level


def bell_draw(stream_key, extent, spread, limit, split=(), kind=jnp.bfloat16):
    factor_of = block_scale(stream_key, extent, split, -0.22, 0.18) if split else 1.0
    entries = jax.random.normal(stream_key, extent, jnp.float32) * spread * factor_of
    return jnp.minimum(jnp.maximum(entries, -limit), limit).astype(kind)


def setup_inputs(seed: int = 0) -> dict:
    keys = jax.random.split(jax.random.key(seed), 19)
    return {
        "block_input": draw_block_input(jax.random.fold_in(keys[18], 71), 0),
        "cotangent": bell_draw(keys[1], (TOKENS, D), 1.0, 6.0, ((0, 8), (1, 4))),
        "image_ids": draw_image_ids(jax.random.fold_in(keys[18], 71), 0),
        "qkv_weight": draw_qkv_weight(jax.random.fold_in(keys[18], 71), 0),
        "proj_weight": bell_draw(keys[4], (D, D), (D // 64) ** -0.5, 1.5, ((0, 4), (1, 8))),
        "fc1_weight": bell_draw(keys[5], (FF, D), D ** -0.5, 0.1875, ((0, 4), (1, 8))),
        "fc2_weight": bell_draw(keys[6], (FF, D), FF ** -0.5, 0.09375, ((0, 4), (1, 8))),
        "norm1_gain": jnp.clip(1.0 + 0.15 * jax.random.normal(keys[7], (D,), jnp.float32), 0.25, 1.75),
        "norm1_shift": bell_draw(keys[8], (D,), 0.5, 3.0, ((0, 4),), jnp.float32),
        "q_bias": bell_draw(keys[9], (D,), 0.5, 3.0, ((0, 4),), jnp.float32),
        "v_bias": bell_draw(keys[10], (D,), 0.5, 3.0, ((0, 4),), jnp.float32),
        "proj_bias": bell_draw(keys[11], (D,), 0.5, 3.0, ((0, 4),), jnp.float32),
        "scale_attn": jnp.clip(jnp.exp(math.log(2.0) - 1.3862944 * jax.random.uniform(keys[12], (D,), jnp.float32) ** block_scale(keys[12], (D,), ((0, 4),), -0.2, 0.2)), 0.5, 2.0),
        "norm2_gain": jnp.clip(1.0 + 0.15 * jax.random.normal(keys[13], (D,), jnp.float32), 0.25, 1.75),
        "norm2_shift": bell_draw(keys[14], (D,), 0.5, 3.0, ((0, 4),), jnp.float32),
        "fc1_bias": bell_draw(keys[15], (FF,), 0.5, 3.0, ((0, 4),), jnp.float32),
        "fc2_bias": bell_draw(keys[16], (D,), 0.5, 3.0, ((0, 4),), jnp.float32),
        "scale_mlp": jnp.clip(jnp.exp(math.log(2.0) - 1.3862944 * jax.random.uniform(keys[17], (D,), jnp.float32) ** block_scale(keys[17], (D,), ((0, 4),), -0.2, 0.2)), 0.5, 2.0),
    }


EPS = 1e-06
NEG = -1e+30
HIGH = lax.Precision.HIGHEST

@jax.custom_vjp
def low(v):
    return lax.optimization_barrier(v.astype(jnp.bfloat16)).astype(jnp.float32)

@jax.custom_vjp
def low_back(v):
    return v

def low_keep(v):
    return (low(v), None)

def low_pass(kept, grad):
    return (grad,)

def back_keep(v):
    return (v, None)

def back_low(kept, grad):
    return (low(grad),)
low.defvjp(low_keep, low_pass)
low_back.defvjp(back_keep, back_low)

def layer_norm(value, gain, shift):
    mean = lax.optimization_barrier(jnp.mean(value, axis=-1, keepdims=True))
    square = lax.optimization_barrier(jnp.mean(value * value, axis=-1, keepdims=True))
    scaled = (value - mean) * lax.rsqrt(square - mean * mean + EPS)
    return scaled * gain + shift

def times_t(left, right):
    return lax.dot_general(left, right, (((1,), (1,)), ((), ())), precision=HIGH, preferred_element_type=jnp.float32)

def attention(query, key_all, value_all, image_ids):
    scale = HEAD_DIM ** (-0.5)
    margin = REACH * TOK_DEV
    span = (2 * REACH + 1) * TOK_DEV
    fill_ids = -jnp.ones((margin,), jnp.int32)
    id_padded = jnp.concatenate([fill_ids, image_ids.astype(jnp.int32), fill_ids])
    zeros = jnp.zeros((margin, D), jnp.float32)
    key_padded = jnp.concatenate([zeros, key_all, zeros])
    value_padded = jnp.concatenate([zeros, value_all, zeros])

    def one_block(start):
        q_rows = lax.dynamic_slice_in_dim(query, start, TOK_DEV, 0).reshape(TOK_DEV, HEADS, HEAD_DIM)
        k_rows = lax.dynamic_slice_in_dim(key_padded, start, span, 0).reshape(span, HEADS, HEAD_DIM)
        v_rows = lax.dynamic_slice_in_dim(value_padded, start, span, 0).reshape(span, HEADS, HEAD_DIM)
        q_ids = lax.dynamic_slice_in_dim(image_ids.astype(jnp.int32), start, TOK_DEV, 0)
        k_ids = lax.dynamic_slice_in_dim(id_padded, start, span, 0)
        valid = (q_ids >= 0)[None, :, None]
        allowed = (q_ids[:, None] == k_ids[None, :])[None] & valid
        score = low_back(jnp.einsum('qhd,khd->hqk', q_rows, k_rows, precision=HIGH) * scale)
        masked = jnp.where(allowed, score, NEG)
        peak = lax.optimization_barrier(jnp.max(masked, axis=-1, keepdims=True))
        expon = jnp.where(allowed, jnp.exp(masked - peak), 0.0)
        total = jnp.where(valid, lax.optimization_barrier(jnp.sum(expon, axis=-1, keepdims=True)), 1.0)
        prob = low(expon / total)
        return jnp.einsum('hqk,khd->qhd', prob, v_rows, precision=HIGH).reshape(TOK_DEV, D)
    starts = jnp.arange(N_SEQ, dtype=jnp.int32) * TOK_DEV
    return lax.map(jax.checkpoint(one_block), starts).reshape(TOKENS, D)

def forward(params, image_ids):
    block_input, qkv_weight, proj_weight, fc1_weight, fc2_weight, norm1_gain, norm1_shift, q_bias, v_bias, proj_bias, scale_attn, norm2_gain, norm2_shift, fc1_bias, fc2_bias, scale_mlp = params
    normed1 = low(layer_norm(block_input, norm1_gain, norm1_shift))
    weight3 = qkv_weight.reshape(D, 3, D)
    query = low_back(low(times_t(normed1, weight3[:, 0]) + q_bias))
    key_all = low_back(low(times_t(normed1, weight3[:, 1])))
    value_all = low_back(low(times_t(normed1, weight3[:, 2]) + v_bias))
    context = low_back(low(attention(query, key_all, value_all, image_ids)))
    branch = low_back(jnp.dot(context, proj_weight, precision=HIGH, preferred_element_type=jnp.float32))
    middle = block_input + scale_attn * (branch + proj_bias)
    normed2 = low(layer_norm(middle, norm2_gain, norm2_shift))
    before = low_back(times_t(normed2, fc1_weight) + fc1_bias)
    hidden = low(jax.nn.gelu(before, approximate=False))
    second = low_back(jnp.dot(hidden, fc2_weight, precision=HIGH, preferred_element_type=jnp.float32))
    return middle + scale_mlp * (second + fc2_bias)

def reference(block_input, cotangent, image_ids, qkv_weight, proj_weight, fc1_weight, fc2_weight, norm1_gain, norm1_shift, q_bias, v_bias, proj_bias, scale_attn, norm2_gain, norm2_shift, fc1_bias, fc2_bias, scale_mlp):
    floats = (block_input.astype(jnp.float32), qkv_weight.astype(jnp.float32), proj_weight.astype(jnp.float32), fc1_weight.astype(jnp.float32), fc2_weight.astype(jnp.float32), norm1_gain.astype(jnp.float32), norm1_shift.astype(jnp.float32), q_bias.astype(jnp.float32), v_bias.astype(jnp.float32), proj_bias.astype(jnp.float32), scale_attn.astype(jnp.float32), norm2_gain.astype(jnp.float32), norm2_shift.astype(jnp.float32), fc1_bias.astype(jnp.float32), fc2_bias.astype(jnp.float32), scale_mlp.astype(jnp.float32))

    def wrapped(params):
        return forward(params, image_ids)
    output, pull = jax.vjp(wrapped, floats)
    grads = pull(cotangent.astype(jnp.float32))[0]
    return (output.astype(jnp.bfloat16), grads[0].astype(jnp.bfloat16), grads[1], grads[2], grads[3], grads[4], grads[5], grads[6], grads[7], grads[8], grads[9], grads[10], grads[11], grads[12], grads[13], grads[14], grads[15])
```

```python
import functools

import jax
import jax.numpy as jnp
from jax import lax
from jax.experimental import pallas as pl
from jax.experimental.pallas import tpu as pltpu
from jax.sharding import PartitionSpec as P

HEAD_DIM = 64
IMG = 1370
IMG_LEAST = 686
EPS = 1e-06
NEG = -1e30
BF = jnp.bfloat16
F32 = jnp.float32
TILE = 256
PAIR = 2 * HEAD_DIM
SCALE = HEAD_DIM ** (-0.5)
INV_SQRT2 = 0.7071067811865476
INV_SQRT2PI = 0.3989422804014327


def px(value, bits):
    pairs = [(i, i ^ bits) for i in range(lax.axis_size("tensor"))]
    return lax.ppermute(value, "tensor", pairs)


def ps(value, bits):
    pairs = [(i, i ^ bits) for i in range(lax.axis_size("seq"))]
    return lax.ppermute(value, "seq", pairs)


def passed_along(block, distance):
    devices = range(lax.axis_size("seq"))
    route = [(i - distance, i) for i in devices if i - distance in devices]
    return lax.ppermute(block, "seq", route)


def gather4(value):
    across = px(value, 2)
    return [value, px(value, 1), across, px(across, 1)]


def swap4(pieces):
    return [pieces[0]] + [px(pieces[r], r) for r in range(1, 4)]


def rows_at(value, index, size):
    return lax.dynamic_slice_in_dim(value, index * size, size, 0)


def unxor(pieces, t):
    low = (t & 1) == 1
    high = (t & 2) == 2
    first = [jnp.where(low, pieces[r ^ 1], pieces[r]) for r in range(4)]
    return [jnp.where(high, first[r ^ 2], first[r]) for r in range(4)]


def nt(left, right):
    return lax.dot_general(left, right, (((1,), (1,)), ((), ())), preferred_element_type=F32)


def nn(left, right):
    return lax.dot_general(left, right, (((1,), (0,)), ((), ())), preferred_element_type=F32)


def tn(left, right):
    return lax.dot_general(left, right, (((0,), (0,)), ((), ())), preferred_element_type=F32)


def params(n=1, limit=56):
    return pltpu.CompilerParams(
        dimension_semantics=("arbitrary",) * n, vmem_limit_bytes=limit * 1024 * 1024
    )


def stats_of(chunks, width):
    total = sum(jnp.sum(c, axis=1, keepdims=True) for c in chunks)
    square = sum(jnp.sum(c * c, axis=1, keepdims=True) for c in chunks)
    mean = total / width
    rstd = lax.rsqrt(square / width - mean * mean + EPS)
    return mean, rstd


def qkv_kernel(sc, x0, x1, x2, x3, w_ref, vec, qb, vb, n1_ref, q_ref, kv0_ref, kv1_ref, wout, wscr):
    groups = w_ref.shape[0]
    part = w_ref.shape[2]
    features = w_ref.shape[1]

    @pl.when(pl.program_id(0) == 0)
    def _():
        for g in range(groups):
            wscr[:, g * part : (g + 1) * part] = w_ref[g]
        wout[...] = wscr[...]

    t = sc[0]
    chunks = unxor([r[...].astype(F32) for r in (x0, x1, x2, x3)], t)
    fw = x0.shape[1]
    width = 4 * fw
    mean, rstd = stats_of(chunks, width)
    for a in range(4):
        lo = a * fw
        scaled = (chunks[a] - mean) * rstd
        n1_ref[:, lo : lo + fw] = (
            scaled * vec[0:1, lo : lo + fw] + vec[1:2, lo : lo + fw]
        ).astype(BF)
    normed = n1_ref[...]
    query = nt(normed, wscr[:, 0:width]) + qb[...]
    q_ref[...] = query.astype(BF)
    key = nt(normed, wscr[:, width : 2 * width]).astype(BF)
    value = (nt(normed, wscr[:, 2 * width : 3 * width]) + vb[...]).astype(BF)
    for p, ref in enumerate((kv0_ref, kv1_ref)):
        ref[:, 0:PAIR] = key[:, p * PAIR : (p + 1) * PAIR]
        ref[:, PAIR : 2 * PAIR] = value[:, p * PAIR : (p + 1) * PAIR]


def qkv_call(sc, xs, w, vec, qb, vb):
    rows, fw = xs[0].shape
    groups, features, part = w.shape
    width = 4 * fw
    tile = TILE

    def full(shape):
        return pl.BlockSpec(shape, lambda i, sc: (0,) * len(shape))

    def row(n):
        return pl.BlockSpec((tile, n), lambda i, sc: (i, 0))

    return pl.pallas_call(
        qkv_kernel,
        grid_spec=pltpu.PrefetchScalarGridSpec(
            num_scalar_prefetch=1,
            grid=(rows // tile,),
            in_specs=[row(fw)] * 4
            + [full(w.shape), full(vec.shape), full(qb.shape), full(vb.shape)],
            out_specs=[
                row(width),
                row(features),
                row(2 * PAIR),
                row(2 * PAIR),
                full((features, groups * part)),
            ],
            scratch_shapes=[pltpu.VMEM((features, groups * part), BF)],
        ),
        out_shape=[
            jax.ShapeDtypeStruct((rows, width), BF),
            jax.ShapeDtypeStruct((rows, features), BF),
            jax.ShapeDtypeStruct((rows, 2 * PAIR), BF),
            jax.ShapeDtypeStruct((rows, 2 * PAIR), BF),
            jax.ShapeDtypeStruct((features, groups * part), BF),
        ],
        compiler_params=params(),
        name="qkv",
    )(sc, *xs, w, vec, qb, vb)


def load_pieces(pieces, target, sem, offsets, counts):
    copies = [
        pltpu.make_async_copy(ref, target.at[pl.ds(offset, count), :], sem.at[k])
        for k, (ref, offset, count) in enumerate(zip(pieces, offsets, counts))
    ]
    for copy in copies:
        copy.start()
    for copy in copies:
        copy.wait()


def head_lanes(shape, head):
    lane = lax.broadcasted_iota(jnp.int32, shape, 1)
    return (lane >= head * HEAD_DIM) & (lane < (head + 1) * HEAD_DIM)


def scores_of(kv, head_query, j, start, end):
    raw = nt(kv[pl.ds(pl.multiple_of(j * TILE, TILE), TILE), 0:PAIR], head_query)
    place = lax.broadcasted_iota(jnp.int32, raw.shape, 0) + j * TILE
    return jnp.where((place >= start) & (place < end), raw, NEG)


def fold8(values, how):
    return how(values.reshape(values.shape[0] // 8, 8, values.shape[1]), axis=0)


def fwd_kernel(offsets, counts, sc, q_ref, se_ref, *refs):
    n = len(counts)
    pieces = refs[:n]
    ctx_ref, st_ref, kv, s_scr, acc, sem = refs[n:]
    i = pl.program_id(0)

    @pl.when(i == 0)
    def _():
        load_pieces(pieces, kv, sem, offsets, counts)

    lo = sc[1 + 2 * i]
    hi = sc[2 + 2 * i]
    start = se_ref[0:1, :]
    end = se_ref[1:2, :]
    query = q_ref[...].astype(F32) * SCALE
    for head in range(2):
        head_query = jnp.where(head_lanes(query.shape, head), query, 0.0).astype(BF)

        def first(j, peak):
            score = scores_of(kv, head_query, j, start, end)
            s_scr[j - lo] = score
            return jnp.maximum(peak, fold8(score, jnp.max))

        peak8 = lax.fori_loop(lo, hi, first, jnp.full((8, TILE), NEG, F32))
        peak = jnp.max(peak8, axis=0, keepdims=True)
        peak = jnp.maximum(peak, 0.1 * NEG)

        def second(j, total):
            expon = jnp.exp(s_scr[j - lo] - peak)
            s_scr[j - lo] = expon
            return total + fold8(expon, jnp.sum)

        total8 = lax.fori_loop(lo, hi, second, jnp.zeros((8, TILE), F32))
        total = jnp.sum(total8, axis=0, keepdims=True)
        inverse = 1.0 / jnp.where(end > start, total, 1.0)
        acc[head] = jnp.zeros(acc.shape[1:], F32)

        def third(j, carry):
            prob = (s_scr[j - lo] * inverse).astype(BF)
            vals = kv[pl.ds(pl.multiple_of(j * TILE, TILE), TILE), PAIR : 2 * PAIR]
            acc[head] += tn(vals, prob)
            return carry

        lax.fori_loop(lo, hi, third, 0)
        st_ref[head : head + 1, :] = peak
        st_ref[2 + head : 3 + head, :] = inverse
    both = jnp.concatenate([acc[0, 0:HEAD_DIM, :], acc[1, HEAD_DIM:PAIR, :]], axis=0)
    ctx_ref[...] = both.T.astype(BF)


def fwd_call(pair, sc, query, spans, pieces, offsets, counts):
    rows = query.shape[0]
    near = sum(counts)
    return pl.pallas_call(
        functools.partial(fwd_kernel, offsets, counts),
        grid_spec=pltpu.PrefetchScalarGridSpec(
            num_scalar_prefetch=1,
            grid=(rows // TILE,),
            in_specs=[
                pl.BlockSpec((TILE, PAIR), lambda i, sc: (i, pair)),
                pl.BlockSpec((8, TILE), lambda i, sc: (0, i)),
            ]
            + [pl.BlockSpec(memory_space=pl.ANY)] * len(pieces),
            out_specs=[
                pl.BlockSpec((TILE, PAIR), lambda i, sc: (i, 0)),
                pl.BlockSpec((8, TILE), lambda i, sc: (0, i)),
            ],
            scratch_shapes=[
                pltpu.VMEM((near, 2 * PAIR), BF),
                pltpu.VMEM((near // TILE, TILE, TILE), F32),
                pltpu.VMEM((2, PAIR, TILE), F32),
                pltpu.SemaphoreType.DMA((len(pieces),)),
            ],
        ),
        out_shape=[
            jax.ShapeDtypeStruct((rows, PAIR), BF),
            jax.ShapeDtypeStruct((8, rows), F32),
        ],
        compiler_params=params(),
        name="attn_fwd",
    )(sc, query, spans, *pieces)


def bwd_kernel(offsets, counts, own, sc, q_ref, se_ref, st_ref, g_ref, *refs):
    n = len(counts)
    pieces = refs[:n]
    dq_ref = refs[n]
    outs = refs[n + 1 : 2 * n + 1]
    kv, w_scr, g_scr, acc, dq_scr, sem = refs[2 * n + 1 :]
    r = pl.program_id(0)

    @pl.when(r == 0)
    def _():
        load_pieces(pieces, kv, sem, offsets, counts)
        acc[...] = jnp.zeros(acc.shape, F32)

    i = sc[0] ^ r
    lo = sc[1 + 2 * i]
    hi = sc[2 + 2 * i]
    start = se_ref[0:1, :]
    end = se_ref[1:2, :]
    query = q_ref[...].astype(F32) * SCALE
    grad = g_ref[0].astype(F32)
    for head in range(2):
        lanes = head_lanes(query.shape, head)
        head_query = jnp.where(lanes, query, 0.0).astype(BF)
        head_grad = jnp.where(lanes, grad, 0.0).astype(BF)
        peak = st_ref[head : head + 1, :]
        inverse = st_ref[2 + head : 3 + head, :]

        def first(j, dot8):
            score = scores_of(kv, head_query, j, start, end)
            weight = jnp.exp(score - peak) * inverse
            vals = kv[pl.ds(pl.multiple_of(j * TILE, TILE), TILE), PAIR : 2 * PAIR]
            grad_prob = nt(vals, head_grad)
            w_scr[j - lo] = weight
            g_scr[j - lo] = grad_prob
            return dot8 + fold8(weight * grad_prob, jnp.sum)

        dot8 = lax.fori_loop(lo, hi, first, jnp.zeros((8, TILE), F32))
        rowdot = jnp.sum(dot8, axis=0, keepdims=True)
        dq_scr[head] = jnp.zeros(dq_scr.shape[1:], F32)

        def second(j, carry):
            weight = w_scr[j - lo]
            grad_score = (weight * (g_scr[j - lo] - rowdot)).astype(BF)
            prob = weight.astype(BF)
            at = pl.ds(pl.multiple_of(j * TILE, TILE), TILE)
            acc[at, 0:PAIR] += nn(grad_score, head_query)
            acc[at, PAIR : 2 * PAIR] += nn(prob, head_grad)
            dq_scr[head] += tn(kv[at, 0:PAIR], grad_score)
            return carry

        lax.fori_loop(lo, hi, second, 0)
    both = jnp.concatenate([dq_scr[0, 0:HEAD_DIM, :], dq_scr[1, HEAD_DIM:PAIR, :]], axis=0)
    dq_ref[...] = (both.T * SCALE).astype(BF)

    @pl.when(r == pl.num_programs(0) - 1)
    def _():
        for k in range(n):
            piece = acc[offsets[k] : offsets[k] + counts[k], :]
            outs[k][...] = piece.astype(outs[k].dtype)


def bwd_call(pair, sc, query, spans, stats, grads, pieces, offsets, counts, own):
    rows = query.shape[0]
    near = sum(counts)

    def whole(count):
        return pl.BlockSpec((count, 2 * PAIR), lambda r, sc: (0, 0))

    return pl.pallas_call(
        functools.partial(bwd_kernel, offsets, counts, own),
        grid_spec=pltpu.PrefetchScalarGridSpec(
            num_scalar_prefetch=1,
            grid=(rows // TILE,),
            in_specs=[
                pl.BlockSpec((TILE, PAIR), lambda r, sc: (sc[0] ^ r, pair)),
                pl.BlockSpec((8, TILE), lambda r, sc: (0, sc[0] ^ r)),
                pl.BlockSpec((8, TILE), lambda r, sc: (0, sc[0] ^ r)),
                pl.BlockSpec((1, TILE, PAIR), lambda r, sc: (r, 0, pair)),
            ]
            + [pl.BlockSpec(memory_space=pl.ANY)] * len(pieces),
            out_specs=[pl.BlockSpec((TILE, PAIR), lambda r, sc: (sc[0] ^ r, 0))]
            + [whole(c) for c in counts],
            scratch_shapes=[
                pltpu.VMEM((near, 2 * PAIR), BF),
                pltpu.VMEM((near // TILE, TILE, TILE), F32),
                pltpu.VMEM((near // TILE, TILE, TILE), F32),
                pltpu.VMEM((near, 2 * PAIR), F32),
                pltpu.VMEM((2, PAIR, TILE), F32),
                pltpu.SemaphoreType.DMA((len(pieces),)),
            ],
        ),
        out_shape=[jax.ShapeDtypeStruct((rows, PAIR), BF)]
        + [
            jax.ShapeDtypeStruct((c, 2 * PAIR), F32 if k == own else BF)
            for k, c in enumerate(counts)
        ],
        compiler_params=params(),
        name="attn_bwd",
    )(sc, query, spans, stats, grads, *pieces)


def whole_spec(shape):
    return pl.BlockSpec(shape, lambda i, sc: (0,) * len(shape))


def proj_kernel(sc, c0, c1, c2, c3, w0, w1, w2, w3, x0, x1, x2, x3, vec, bt_ref, mid_ref, n2_ref):
    t = sc[0]
    fw = x0.shape[1]
    branch = vec[4:5, :] + sum(
        nn(c[...], w[...]) for c, w in ((c0, w0), (c1, w1), (c2, w2), (c3, w3))
    )
    bt_ref[...] = branch
    chunks = unxor([x[...].astype(F32) for x in (x0, x1, x2, x3)], t)
    for a in range(4):
        at = slice(a * fw, (a + 1) * fw)
        mid_ref[:, at] = chunks[a] + vec[5:6, at] * branch[:, at]
    middle = mid_ref[...]
    mean, rstd = stats_of([middle], 4 * fw)
    n2_ref[...] = ((middle - mean) * rstd * vec[2:3, :] + vec[3:4, :]).astype(BF)


def proj_call(sc, contexts, ws, xs, vec):
    rows, fw = contexts[0].shape
    width = ws[0].shape[1]
    tile = rows // 2

    def row(n):
        return pl.BlockSpec((tile, n), lambda i, sc: (i, 0))

    def mine(n):
        return pl.BlockSpec((tile, n), lambda i, sc: (sc[0] * 2 + i, 0))

    return pl.pallas_call(
        proj_kernel,
        grid_spec=pltpu.PrefetchScalarGridSpec(
            num_scalar_prefetch=1,
            grid=(2,),
            in_specs=[row(fw)] * 4
            + [whole_spec(ws[0].shape)] * 4
            + [mine(fw)] * 4
            + [whole_spec(vec.shape)],
            out_specs=[row(width)] * 3,
        ),
        out_shape=[
            jax.ShapeDtypeStruct((rows, width), F32),
            jax.ShapeDtypeStruct((rows, width), F32),
            jax.ShapeDtypeStruct((rows, width), BF),
        ],
        compiler_params=params(),
        name="proj",
    )(sc, *contexts, *ws, *xs, vec)


def mlp_kernel(n0, n1, g0, g1, fc1, fc2, bias, h_ref, gb_ref, s0, s1, d0, d1, fb_ref):
    i = pl.program_id(0)
    step = 256
    hidden_units = fc1.shape[0]

    @pl.when(i == 0)
    def _():
        fb_ref[...] = jnp.zeros(fb_ref.shape, F32)

    def work(n_ref, g_ref, s_ref, d_ref):
        normed = n_ref[...]
        grads = g_ref[...]
        for u in range(hidden_units // step):
            at = slice(u * step, (u + 1) * step)
            before = nt(normed, fc1[at, :]) + bias[:, at]
            phi = 0.5 * (1.0 + lax.erf(before * INV_SQRT2))
            h_ref[:, at] = (before * phi).astype(BF)
            slope = phi + before * (jnp.exp(-0.5 * before * before) * INV_SQRT2PI)
            grad_before = (slope * nt(grads, fc2[at, :])).astype(BF)
            gb_ref[:, at] = grad_before
            wide = grad_before.astype(F32)
            fb_ref[0:1, at] += jnp.sum(wide, axis=0, keepdims=True)
        d_ref[...] = nn(gb_ref[...], fc1[...]).astype(BF)
        s_ref[...] = nn(h_ref[...], fc2[...]).astype(BF)

    @pl.when(i == 0)
    def _():
        work(n0, g0, s0, d0)

    @pl.when(i == 1)
    def _():
        work(n1, g1, s1, d1)


def mlp_call(normed, grads, weights, bias):
    rows, width = normed[0].shape
    hidden_units = bias.shape[1]

    def full(shape):
        return pl.BlockSpec(shape, lambda i: (0,) * len(shape))

    piece = jax.ShapeDtypeStruct((rows, width), BF)
    return pl.pallas_call(
        mlp_kernel,
        grid=(2,),
        in_specs=[full((rows, width))] * 4
        + [
            pl.BlockSpec((hidden_units, width), lambda i: (0, 0)),
            pl.BlockSpec((hidden_units, width), lambda i: (1, 0)),
            full(bias.shape),
        ],
        out_specs=[pl.BlockSpec((rows, hidden_units), lambda i: (i, 0))] * 2
        + [full((rows, width))] * 4
        + [full((8, hidden_units))],
        out_shape=[jax.ShapeDtypeStruct((2 * rows, hidden_units), BF)] * 2
        + [piece] * 4
        + [jax.ShapeDtypeStruct((8, hidden_units), F32)],
        compiler_params=params(),
        name="mlp",
    )(*normed, *grads, weights, weights, bias)


def mid_kernel(
    sc, a0, a1, a2, k0, k1, k2, k3, mid, bt, w0, w1, w2, w3, vec, gm_ref, gb_ref, gc_ref, sums
):
    t = sc[0]
    fw = k0.shape[1]
    width = 4 * fw

    @pl.when(pl.program_id(0) == 0)
    def _():
        sums[...] = jnp.zeros(sums.shape, F32)

    grad_normed = a0[...].astype(F32) + a1[...].astype(F32) + a2[...].astype(F32)
    middle = mid[...]
    mean, rstd = stats_of([middle], width)
    scaled = (middle - mean) * rstd
    inner = grad_normed * vec[2:3, :]
    mean_a = jnp.sum(inner, axis=1, keepdims=True) / width
    mean_b = jnp.sum(inner * scaled, axis=1, keepdims=True) / width
    chunks = unxor([k[...].astype(F32) for k in (k0, k1, k2, k3)], t)
    back = rstd * (inner - mean_a - scaled * mean_b)
    for a in range(4):
        at = slice(a * fw, (a + 1) * fw)
        gm_ref[:, at] = chunks[a] + back[:, at]
    grad_middle = gm_ref[...]
    grad_branch = grad_middle * vec[5:6, :]
    small = grad_branch.astype(BF)
    gb_ref[...] = small
    for r, w in enumerate((w0, w1, w2, w3)):
        gc_ref[r] = nt(small, w[...]).astype(BF)

    def add(k, values):
        sums[k : k + 1, :] += jnp.sum(values, axis=0, keepdims=True)

    add(0, grad_normed * scaled)
    add(1, grad_normed)
    add(2, grad_middle * bt[...])
    add(3, grad_branch)


def mid_call(sc, parts, cots, middle, branch, ws, vec):
    rows, width = middle.shape
    fw = width // 4
    tile = rows // 2

    def row(n):
        return pl.BlockSpec((tile, n), lambda i, sc: (i, 0))

    return pl.pallas_call(
        mid_kernel,
        grid_spec=pltpu.PrefetchScalarGridSpec(
            num_scalar_prefetch=1,
            grid=(2,),
            in_specs=[row(width)] * 3
            + [row(fw)] * 4
            + [row(width)] * 2
            + [whole_spec(ws[0].shape)] * 4
            + [whole_spec(vec.shape)],
            out_specs=[
                row(width),
                row(width),
                pl.BlockSpec((4, tile, fw), lambda i, sc: (0, i, 0)),
                whole_spec((8, width)),
            ],
        ),
        out_shape=[
            jax.ShapeDtypeStruct((rows, width), F32),
            jax.ShapeDtypeStruct((rows, width), BF),
            jax.ShapeDtypeStruct((4, rows, fw), BF),
            jax.ShapeDtypeStruct((8, width), F32),
        ],
        compiler_params=params(),
        name="mid",
    )(sc, *parts, *cots, middle, branch, *ws, vec)


def gn1_kernel(sc, gq0, gq1, gk, gv, w_ref, o0, o1, o2, o3):
    width = w_ref.shape[1] // 3
    query = jnp.concatenate([gq0[...], gq1[...]], axis=1)
    total = (
        nn(query, w_ref[:, 0:width])
        + nn(gk[...], w_ref[:, width : 2 * width])
        + nn(gv[...], w_ref[:, 2 * width : 3 * width])
    ).astype(BF)
    for r, ref in enumerate((o0, o1, o2, o3)):

        @pl.when(pl.program_id(0) == r)
        def _():
            ref[...] = total


def gn1_call(sc, gq0, gq1, gk, gv, w):
    rows = gk.shape[0]
    features, wide = w.shape
    sub = rows // 4

    def row(n):
        return pl.BlockSpec((sub, n), lambda r, sc: (sc[0] ^ r, 0))

    return pl.pallas_call(
        gn1_kernel,
        grid_spec=pltpu.PrefetchScalarGridSpec(
            num_scalar_prefetch=1,
            grid=(4,),
            in_specs=[row(PAIR), row(PAIR), row(features), row(features), whole_spec(w.shape)],
            out_specs=[whole_spec((sub, wide // 3))] * 4,
        ),
        out_shape=[jax.ShapeDtypeStruct((sub, wide // 3), BF)] * 4,
        compiler_params=params(),
        name="gn1",
    )(sc, gq0, gq1, gk, gv, w)


def last_kernel(sc, a0, a1, a2, x0, x1, x2, x3, gm, vec, o0, o1, o2, o3, sums, scr):
    t = sc[0]
    fw = x0.shape[1]
    width = 4 * fw

    @pl.when(pl.program_id(0) == 0)
    def _():
        sums[...] = jnp.zeros(sums.shape, F32)

    grad_normed = a0[...].astype(F32) + a1[...].astype(F32) + a2[...].astype(F32)
    chunks = unxor([x[...].astype(F32) for x in (x0, x1, x2, x3)], t)
    value = jnp.concatenate(chunks, axis=1)
    mean, rstd = stats_of([value], width)
    scaled = (value - mean) * rstd
    inner = grad_normed * vec[0:1, :]
    mean_a = jnp.sum(inner, axis=1, keepdims=True) / width
    mean_b = jnp.sum(inner * scaled, axis=1, keepdims=True) / width
    scr[...] = (gm[...] + rstd * (inner - mean_a - scaled * mean_b)).astype(BF)
    for r, ref in enumerate((o0, o1, o2, o3)):
        ref[...] = scr[:, pl.ds(pl.multiple_of((t ^ r) * fw, fw), fw)]
    sums[0:1, :] += jnp.sum(grad_normed * scaled, axis=0, keepdims=True)
    sums[1:2, :] += jnp.sum(grad_normed, axis=0, keepdims=True)


def last_call(sc, parts, xs, grad_middle, vec):
    rows, width = grad_middle.shape
    fw = width // 4
    tile = rows // 2

    def row(n):
        return pl.BlockSpec((tile, n), lambda i, sc: (i, 0))

    def mine(n):
        return pl.BlockSpec((tile, n), lambda i, sc: (sc[0] * 2 + i, 0))

    return pl.pallas_call(
        last_kernel,
        grid_spec=pltpu.PrefetchScalarGridSpec(
            num_scalar_prefetch=1,
            grid=(2,),
            in_specs=[row(width)] * 3 + [mine(fw)] * 4 + [row(width), whole_spec(vec.shape)],
            out_specs=[row(fw)] * 4 + [whole_spec((8, width))],
            scratch_shapes=[pltpu.VMEM((tile, width), BF)],
        ),
        out_shape=[jax.ShapeDtypeStruct((rows, fw), BF)] * 4
        + [jax.ShapeDtypeStruct((8, width), F32)],
        compiler_params=params(),
        name="last",
    )(sc, *parts, *xs, grad_middle, vec)


def out_kernel(sc, a0, a1, a2, k0, k1, k2, k3, mid, vec, o0, o1, o2, o3, sums, scr):
    t = sc[0]
    fw = k0.shape[1]

    @pl.when(pl.program_id(0) == 0)
    def _():
        sums[...] = jnp.zeros(sums.shape, F32)

    total = a0[...].astype(F32) + a1[...].astype(F32) + a2[...].astype(F32) + vec[6:7, :]
    scr[...] = (mid[...] + vec[7:8, :] * total).astype(BF)
    for r, ref in enumerate((o0, o1, o2, o3)):
        ref[...] = scr[:, pl.ds(pl.multiple_of((t ^ r) * fw, fw), fw)]
    grad = jnp.concatenate(unxor([k[...].astype(F32) for k in (k0, k1, k2, k3)], t), axis=1)
    sums[0:1, :] += jnp.sum(grad * total, axis=0, keepdims=True)
    sums[1:2, :] += jnp.sum(grad * vec[7:8, :], axis=0, keepdims=True)


def out_call(sc, parts, cots, middle, vec):
    rows, width = middle.shape
    fw = width // 4
    tile = rows // 2

    def row(n):
        return pl.BlockSpec((tile, n), lambda i, sc: (i, 0))

    return pl.pallas_call(
        out_kernel,
        grid_spec=pltpu.PrefetchScalarGridSpec(
            num_scalar_prefetch=1,
            grid=(2,),
            in_specs=[row(width)] * 3 + [row(fw)] * 4 + [row(width), whole_spec(vec.shape)],
            out_specs=[row(fw)] * 4 + [whole_spec((8, width))],
            scratch_shapes=[pltpu.VMEM((tile, width), BF)],
        ),
        out_shape=[jax.ShapeDtypeStruct((rows, fw), BF)] * 4
        + [jax.ShapeDtypeStruct((8, width), F32)],
        compiler_params=params(),
        name="block_out",
    )(sc, *parts, *cots, middle, vec)


def placed(pieces, t, axis):
    return jnp.concatenate(unxor(pieces, t), axis=axis)


def reduce4(pieces):
    far = (pieces[2].astype(F32) + px(pieces[3], 1).astype(F32)).astype(BF)
    return pieces[0], px(pieces[1], 1), px(far, 2)


def spans_of(image_ids, row_count, first_row, margin, near):
    tokens = image_ids.shape[0]
    most = tokens // IMG_LEAST + 1
    place = jnp.arange(tokens, dtype=jnp.int32)
    names = jnp.arange(most, dtype=jnp.int32)[:, None]
    same = image_ids[None, :] == names
    low = jnp.min(jnp.where(same, place[None, :], tokens), axis=1)
    high = jnp.max(jnp.where(same, place[None, :] + 1, 0), axis=1)
    own = lax.dynamic_slice_in_dim(image_ids, first_row, row_count, 0)
    mine = own[None, :] == names
    start = jnp.sum(jnp.where(mine, low[:, None], 0), axis=0)
    end = jnp.sum(jnp.where(mine, high[:, None], 0), axis=0)
    valid = own >= 0
    shift = margin - first_row
    start = jnp.where(valid, start + shift, 0)
    end = jnp.where(valid, end + shift, 0)
    lo = jnp.min(jnp.where(valid, start, near).reshape(-1, TILE), axis=1)
    hi = jnp.max(end.reshape(-1, TILE), axis=1)
    lo = jnp.clip(lo // TILE, 0, near // TILE)
    hi = jnp.clip(-(-hi // TILE), 0, near // TILE)
    spans = jnp.concatenate(
        [start[None, :], end[None, :], jnp.zeros((6, row_count), jnp.int32)], axis=0
    )
    return spans, jnp.stack([lo, hi], axis=1).reshape(-1)


def per_device(
    block_input,
    cotangent,
    image_ids,
    qkv_weight,
    proj_weight,
    fc1_weight,
    fc2_weight,
    norm1_gain,
    norm1_shift,
    q_bias,
    v_bias,
    proj_bias,
    scale_attn,
    norm2_gain,
    norm2_shift,
    fc1_bias,
    fc2_bias,
    scale_mlp,
):
    row_count, fw = block_input.shape
    n_seq = lax.axis_size("seq")
    width = 4 * fw
    features = qkv_weight.shape[0]
    sub = row_count // 4
    t = lax.axis_index("tensor").astype(jnp.int32)
    s = lax.axis_index("seq").astype(jnp.int32)
    reach = (IMG - 1 + row_count - 1) // row_count
    tile_rows = min(128, row_count)

    xs = gather4(block_input)
    if n_seq == 8:
        z2, z4, z6 = ps(qkv_weight, 2), ps(qkv_weight, 4), ps(qkv_weight, 6)
        found = [None] * 8
        for bits, piece in ((0, qkv_weight), (2, z2), (4, z4), (6, z6)):
            found[bits] = piece
            found[bits ^ 1] = ps(piece, 1)
        w_qkv = jnp.zeros((8,) + qkv_weight.shape, BF)
        for bits in range(8):
            w_qkv = lax.dynamic_update_slice(w_qkv, found[bits][None], (s ^ bits, 0, 0))
    else:
        w_qkv = lax.all_gather(qkv_weight, "seq", axis=1, tiled=True)[None]
    vec_own = jnp.stack(
        [
            norm1_gain,
            norm1_shift,
            norm2_gain,
            norm2_shift,
            proj_bias,
            scale_attn,
            fc2_bias,
            scale_mlp,
        ]
    )
    vec = placed([vec_own] + [px(vec_own, r) for r in range(1, 4)], t, 1)
    others = lax.all_gather(
        jnp.concatenate([fc1_weight, fc2_weight, proj_weight], axis=0), "seq", axis=1, tiled=True
    )
    units = fc1_weight.shape[0]
    ws = gather4(others[2 * units :])

    offsets_of = []
    counts = []
    for place in range(2 * reach + 1):
        offset = reach - place
        if offset == 0:
            count = row_count
        else:
            need = IMG - 1 - (abs(offset) - 1) * row_count
            count = min(row_count, -(-need // tile_rows) * tile_rows)
        offsets_of.append(offset)
        counts.append(count)
    offsets = [sum(counts[:k]) for k in range(len(counts))]
    near = sum(counts)
    margin = offsets[reach]
    spans, edges = spans_of(image_ids, row_count, s * row_count, margin, near)
    sc = jnp.concatenate([t[None], edges])
    sc_t = t[None]

    normed1, query, kv0, kv1, w_full = qkv_call(
        sc_t, xs, w_qkv, vec, q_bias[None, :], v_bias[None, :]
    )
    nears = []
    for kv in (kv0, kv1):
        pieces = []
        for offset, count in zip(offsets_of, counts):
            if offset == 0:
                pieces.append(kv)
            elif offset > 0:
                pieces.append(passed_along(kv[row_count - count :], offset))
            else:
                pieces.append(passed_along(kv[:count], offset))
        nears.append(pieces)
    cots = swap4([rows_at(cotangent, t ^ r, sub) for r in range(4)])
    grad_second = (
        jnp.concatenate(unxor(cots, t), axis=1).astype(F32) * vec[7:8, :]
    ).astype(BF)
    grads = gather4(grad_second)
    contexts = []
    stats = []
    for pair in range(2):
        ctx, st = fwd_call(pair, sc, query, spans, nears[pair], offsets, counts)
        contexts.append(ctx)
        stats.append(st)
    context = jnp.concatenate(contexts, axis=1)
    ctx_rows = swap4([rows_at(context, t ^ r, sub) for r in range(4)])
    branch, middle, normed2 = proj_call(sc_t, ctx_rows, ws, xs, vec)
    n_near = px(normed2, 1)
    n_across = px(normed2, 2)
    n_far = px(n_across, 1)
    bias1 = fc1_bias[None, :]
    hid_b, gb_b, s2, s3, d2, d3, fb_b = mlp_call((n_across, n_far), grads[2:], others, bias1)
    hid_a, gb_a, s0, s1, d0, d1, fb_a = mlp_call((normed2, n_near), grads[:2], others, bias1)
    parts = reduce4([d0, d1, d2, d3])
    grad_middle, grad_branch, grad_ctx, sums_mid = mid_call(
        sc_t, parts, cots, middle, branch, ws, vec
    )
    swapped = swap4([grad_ctx[r] for r in range(4)])
    grad_rows = jnp.stack(swapped)

    rows_a = jnp.concatenate([normed2, n_near], axis=0)
    rows_b = jnp.concatenate([n_across, n_far], axis=0)
    gs_a = jnp.concatenate(grads[:2], axis=0)
    gs_b = jnp.concatenate(grads[2:], axis=0)
    fc1_part = (tn(gb_a, rows_a) + tn(gb_b, rows_b)).astype(BF)
    fc2_part = (tn(hid_a, gs_a) + tn(hid_b, gs_b)).astype(BF)
    fc_out = lax.psum_scatter(
        jnp.concatenate([fc1_part, fc2_part], axis=0), "seq", scatter_dimension=1, tiled=True
    ).astype(F32)
    o0, o1, o2, o3, sums_out = out_call(sc_t, reduce4([s0, s1, s2, s3]), cots, middle, vec)
    block_output = placed(swap4([o0, o1, o2, o3]), t, 0)
    branch_rows = placed(gather4(grad_branch), t, 0)
    proj_part = tn(context, branch_rows).astype(BF)
    proj_out = lax.psum_scatter(proj_part, "seq", scatter_dimension=1, tiled=True).astype(F32)

    grad_q = []
    grad_k = []
    grad_v = []
    for pair in range(2):
        got = bwd_call(
            pair, sc, query, spans, stats[pair], grad_rows, nears[pair], offsets, counts, reach
        )
        grad_q.append(got[0])
        total = got[1 + reach]
        for k, (offset, count) in enumerate(zip(offsets_of, counts)):
            if offset == 0:
                continue
            back = passed_along(got[1 + k], -offset).astype(F32)
            if count < row_count:
                gap = row_count - count
                ends = ((gap, 0), (0, 0)) if offset > 0 else ((0, gap), (0, 0))
                back = jnp.pad(back, ends)
            total = total + back
        total = total.astype(BF)
        grad_k.append(total[:, :PAIR])
        grad_v.append(total[:, PAIR:])
    gk = jnp.concatenate(grad_k, axis=1)
    gv = jnp.concatenate(grad_v, axis=1)
    gq = jnp.concatenate(grad_q, axis=1)
    pieces = gn1_call(sc_t, grad_q[0], grad_q[1], gk, gv, w_full)
    i0, i1, i2, i3, sums_last = last_call(sc_t, reduce4(pieces), xs, grad_middle, vec)
    input_grad = placed(swap4([i0, i1, i2, i3]), t, 0)
    qkv_parts = [tn(g, normed1) for g in (gq, gk, gv)]
    if n_seq == 8:
        unit = 128
        blocks = jnp.concatenate(
            [
                g.astype(BF).reshape(features, width // unit, unit).transpose(1, 0, 2)
                for g in qkv_parts
            ],
            axis=0,
        ).reshape(2, 2, 2, 3, features, unit)
        for axis, bits in ((1, 2), (1, 1), (0, 4)):
            if bits == 2:
                mine = (s >> 1) & 1
            elif bits == 1:
                mine = s & 1
            else:
                mine = (s >> 2) & 1
            keep = lax.dynamic_index_in_dim(blocks, mine, axis, keepdims=False)
            send = lax.dynamic_index_in_dim(blocks, 1 - mine, axis, keepdims=False)
            blocks = (keep.astype(F32) + ps(send.astype(BF), bits).astype(F32))
        qkv_out = blocks.transpose(1, 0, 2).reshape(features, 3 * unit)
    else:
        qkv_out = lax.psum_scatter(
            jnp.stack(qkv_parts, axis=1).reshape(features, 3 * width).astype(BF),
            "seq",
            scatter_dimension=1,
            tiled=True,
        ).astype(F32)

    rows8 = jnp.concatenate([sums_last[0:2], sums_mid[0:4], sums_out[0:2]], axis=0)
    cut = [lax.dynamic_slice_in_dim(rows8, (t ^ r) * fw, fw, 1) for r in range(4)]
    got = swap4(cut)
    own8 = got[0] + got[1] + got[2] + got[3]
    flat = jnp.concatenate(
        [
            own8.reshape(-1),
            jnp.sum(gq.astype(F32), axis=0),
            jnp.sum(gv.astype(F32), axis=0),
            fb_a[0] + fb_b[0],
        ]
    ).reshape(-1, 128)
    if n_seq == 8:
        for bits in (2, 1, 4):
            flat = flat + ps(flat, bits)
    else:
        flat = lax.psum(flat, "seq")
    flat = flat.reshape(-1)
    own8 = flat[: 8 * fw].reshape(8, fw)
    q_bias_grad = flat[8 * fw : 8 * fw + features]
    v_bias_grad = flat[8 * fw + features : 8 * fw + 2 * features]
    fc1_bias_grad = flat[8 * fw + 2 * features :]
    return (
        block_output,
        input_grad,
        qkv_out,
        proj_out,
        fc_out[:units],
        fc_out[units:],
        own8[0],
        own8[1],
        q_bias_grad,
        v_bias_grad,
        own8[5],
        own8[4],
        own8[2],
        own8[3],
        fc1_bias_grad,
        own8[7],
        own8[6],
    )


def solution(mesh):
    cut = P("tensor", "seq")
    by_tensor = P("tensor")
    in_specs = (P("seq", "tensor"), P("seq", "tensor"), P()) + (cut,) * 4 + (by_tensor,) * 11
    out_specs = (P("seq", "tensor"), P("seq", "tensor")) + (cut,) * 4 + (by_tensor,) * 11
    return jax.shard_map(
        per_device, mesh=mesh, in_specs=in_specs, out_specs=out_specs, check_vma=False
    )
```

```python
import functools

import jax
import jax.numpy as jnp
from jax import lax
from jax.experimental import pallas as pl
from jax.experimental.pallas import tpu as pltpu
from jax.sharding import PartitionSpec as P


HEAD_DIM = 64
IMG = 1370
IMG_LEAST = 686
EPS = 1e-06
NEG = -1e30
BF = jnp.bfloat16
F32 = jnp.float32
TILE = 256
PAIR = 2 * HEAD_DIM
SCALE = HEAD_DIM ** (-0.5)
INV_SQRT2 = 0.7071067811865476
INV_SQRT2PI = 0.3989422804014327


def px(value, bits):
    pairs = [(i, i ^ bits) for i in range(lax.axis_size("tensor"))]
    return lax.ppermute(value, "tensor", pairs)


def ps(value, bits):
    pairs = [(i, i ^ bits) for i in range(lax.axis_size("seq"))]
    return lax.ppermute(value, "seq", pairs)


def passed_along(block, distance):
    devices = range(lax.axis_size("seq"))
    route = [(i - distance, i) for i in devices if i - distance in devices]
    return lax.ppermute(block, "seq", route)


def gather4(value):
    across = px(value, 2)
    return [value, px(value, 1), across, px(across, 1)]


def swap4(pieces):
    return [pieces[0]] + [px(pieces[r], r) for r in range(1, 4)]


def rows_at(value, index, size):
    return lax.dynamic_slice_in_dim(value, index * size, size, 0)


def unxor(pieces, t):
    low = (t & 1) == 1
    high = (t & 2) == 2
    first = [jnp.where(low, pieces[r ^ 1], pieces[r]) for r in range(4)]
    return [jnp.where(high, first[r ^ 2], first[r]) for r in range(4)]


def nt(left, right):
    return lax.dot_general(left, right, (((1,), (1,)), ((), ())), preferred_element_type=F32)


def nn(left, right):
    return lax.dot_general(left, right, (((1,), (0,)), ((), ())), preferred_element_type=F32)


def tn(left, right):
    return lax.dot_general(left, right, (((0,), (0,)), ((), ())), preferred_element_type=F32)


def params(n=1, limit=56):
    return pltpu.CompilerParams(
        dimension_semantics=("arbitrary",) * n, vmem_limit_bytes=limit * 1024 * 1024
    )


def costs(micros):
    return pl.CostEstimate(flops=int(micros * 1e9), transcendentals=0, bytes_accessed=1 << 20)


def stats_of(chunks, width):
    total = sum(jnp.sum(c, axis=1, keepdims=True) for c in chunks)
    square = sum(jnp.sum(c * c, axis=1, keepdims=True) for c in chunks)
    mean = total / width
    rstd = lax.rsqrt(square / width - mean * mean + EPS)
    return mean, rstd


def qkv_kernel(sc, x0, x1, x2, x3, w_ref, vec, qb, vb, n1_ref, q_ref, kv0_ref, kv1_ref, wout, wproj, wscr):
    groups = w_ref.shape[0]
    part = w_ref.shape[2] * 3 // 4
    small = w_ref.shape[2] - part

    @pl.when(pl.program_id(0) == 0)
    def _():
        for g in range(groups):
            wscr[:, g * part : (g + 1) * part] = w_ref[g, :, :part]
            wproj[:, g * small : (g + 1) * small] = w_ref[g, :, part:]
        wout[...] = wscr[...]

    t = sc[0]
    chunks = unxor([r[...].astype(F32) for r in (x0, x1, x2, x3)], t)
    fw = x0.shape[1]
    width = 4 * fw
    mean, rstd = stats_of(chunks, width)
    for a in range(4):
        lo = a * fw
        scaled = (chunks[a] - mean) * rstd
        n1_ref[:, lo : lo + fw] = (
            scaled * vec[0:1, lo : lo + fw] + vec[1:2, lo : lo + fw]
        ).astype(BF)
    normed = n1_ref[...]
    query = nt(normed, wscr[:, 0:width]) + qb[...]
    q_ref[...] = query.astype(BF)
    key = nt(normed, wscr[:, width : 2 * width]).astype(BF)
    value = (nt(normed, wscr[:, 2 * width : 3 * width]) + vb[...]).astype(BF)
    for p, ref in enumerate((kv0_ref, kv1_ref)):
        ref[:, 0:PAIR] = key[:, p * PAIR : (p + 1) * PAIR]
        ref[:, PAIR : 2 * PAIR] = value[:, p * PAIR : (p + 1) * PAIR]


def qkv_call(sc, xs, w, vec, qb, vb):
    rows, fw = xs[0].shape
    groups, features, part = w.shape
    part = part * 3 // 4
    width = 4 * fw
    tile = TILE

    def full(shape):
        return pl.BlockSpec(shape, lambda i, sc: (0,) * len(shape))

    def row(n):
        return pl.BlockSpec((tile, n), lambda i, sc: (i, 0))

    return pl.pallas_call(
        qkv_kernel,
        grid_spec=pltpu.PrefetchScalarGridSpec(
            num_scalar_prefetch=1,
            grid=(rows // tile,),
            in_specs=[row(fw)] * 4
            + [full(w.shape), full(vec.shape), full(qb.shape), full(vb.shape)],
            out_specs=[
                row(width),
                row(features),
                row(2 * PAIR),
                row(2 * PAIR),
                full((features, groups * part)),
                full((features, width)),
            ],
            scratch_shapes=[pltpu.VMEM((features, groups * part), BF)],
        ),
        out_shape=[
            jax.ShapeDtypeStruct((rows, width), BF),
            jax.ShapeDtypeStruct((rows, features), BF),
            jax.ShapeDtypeStruct((rows, 2 * PAIR), BF),
            jax.ShapeDtypeStruct((rows, 2 * PAIR), BF),
            jax.ShapeDtypeStruct((features, groups * part), BF),
            jax.ShapeDtypeStruct((features, width), BF),
        ],
        compiler_params=params(),
        name="qkv",
        cost_estimate=costs(7),
    )(sc, *xs, w, vec, qb, vb)


def load_pieces(pieces, target, sem, offsets, counts):
    copies = [
        pltpu.make_async_copy(ref, target.at[pl.ds(offset, count), :], sem.at[k])
        for k, (ref, offset, count) in enumerate(zip(pieces, offsets, counts))
    ]
    for copy in copies:
        copy.start()
    for copy in copies:
        copy.wait()


def by_head(values):
    lane = lax.broadcasted_iota(jnp.int32, values.shape, 1)
    first = jnp.where(lane < HEAD_DIM, values, 0.0)
    second = jnp.where(lane < HEAD_DIM, 0.0, values)
    return jnp.concatenate([first, second], axis=0).astype(BF)


def joined(values):
    return jnp.concatenate([values[0:HEAD_DIM, :TILE], values[HEAD_DIM:PAIR, TILE:]], axis=0)


def scores_of(kv, head_query, j, start, end):
    raw = nt(kv[pl.ds(pl.multiple_of(j * TILE, TILE), TILE), 0:PAIR], head_query)
    place = lax.broadcasted_iota(jnp.int32, raw.shape, 0) + j * TILE
    return jnp.where((place >= start) & (place < end), raw, NEG)


def fold8(values, how):
    return how(values.reshape(values.shape[0] // 8, 8, values.shape[1]), axis=0)


def twice(row):
    return jnp.concatenate([row, row], axis=1)


def fwd_kernel(offsets, counts, sc, q_ref, se_ref, *refs):
    n = len(counts)
    pieces = refs[:n]
    ctx_ref, st_ref, kv, s_scr, acc, sem = refs[n:]
    i = pl.program_id(0)

    @pl.when(i == 0)
    def _():
        load_pieces(pieces, kv, sem, offsets, counts)

    lo = sc[1 + 2 * i]
    hi = sc[2 + 2 * i]
    start = twice(se_ref[0:1, :])
    end = twice(se_ref[1:2, :])
    head_query = by_head(q_ref[...].astype(F32) * SCALE)

    def first(j, peak):
        score = scores_of(kv, head_query, j, start, end)
        s_scr[j - lo] = score
        return jnp.maximum(peak, fold8(score, jnp.max))

    peak8 = lax.fori_loop(lo, hi, first, jnp.full((8, 2 * TILE), NEG, F32))
    peak = jnp.max(peak8, axis=0, keepdims=True)
    peak = jnp.maximum(peak, 0.1 * NEG)

    def second(j, total):
        expon = jnp.exp(s_scr[j - lo] - peak)
        s_scr[j - lo] = expon
        return total + fold8(expon, jnp.sum)

    total8 = lax.fori_loop(lo, hi, second, jnp.zeros((8, 2 * TILE), F32))
    total = jnp.sum(total8, axis=0, keepdims=True)
    inverse = 1.0 / jnp.where(end > start, total, 1.0)
    acc[...] = jnp.zeros(acc.shape, F32)

    def third(j, carry):
        prob = (s_scr[j - lo] * inverse).astype(BF)
        vals = kv[pl.ds(pl.multiple_of(j * TILE, TILE), TILE), PAIR : 2 * PAIR]
        acc[...] += tn(vals, prob)
        return carry

    lax.fori_loop(lo, hi, third, 0)
    for head in range(2):
        at = slice(head * TILE, (head + 1) * TILE)
        st_ref[head : head + 1, :] = peak[:, at]
        st_ref[2 + head : 3 + head, :] = inverse[:, at]
    ctx_ref[...] = joined(acc[...]).T.astype(BF)


def fwd_call(pair, sc, query, spans, pieces, offsets, counts):
    rows = query.shape[0]
    near = sum(counts)
    return pl.pallas_call(
        functools.partial(fwd_kernel, offsets, counts),
        grid_spec=pltpu.PrefetchScalarGridSpec(
            num_scalar_prefetch=1,
            grid=(rows // TILE,),
            in_specs=[
                pl.BlockSpec((TILE, PAIR), lambda i, sc: (i, pair)),
                pl.BlockSpec((8, TILE), lambda i, sc: (0, i)),
            ]
            + [pl.BlockSpec(memory_space=pl.ANY)] * len(pieces),
            out_specs=[
                pl.BlockSpec((TILE, PAIR), lambda i, sc: (i, 0)),
                pl.BlockSpec((8, TILE), lambda i, sc: (0, i)),
            ],
            scratch_shapes=[
                pltpu.VMEM((near, 2 * PAIR), BF),
                pltpu.VMEM((near // TILE, TILE, 2 * TILE), F32),
                pltpu.VMEM((PAIR, 2 * TILE), F32),
                pltpu.SemaphoreType.DMA((len(pieces),)),
            ],
        ),
        out_shape=[
            jax.ShapeDtypeStruct((rows, PAIR), BF),
            jax.ShapeDtypeStruct((8, rows), F32),
        ],
        compiler_params=params(),
        name="attn_fwd",
        cost_estimate=costs(17),
    )(sc, query, spans, *pieces)


def bwd_kernel(offsets, counts, sc, q_ref, se_ref, st_ref, g_ref, *refs):
    n = len(counts)
    pieces = refs[:n]
    dq_ref = refs[n]
    outs = refs[n + 1 : 2 * n + 1]
    kv, w_scr, g_scr, acc, dq_scr, sem = refs[2 * n + 1 :]
    r = pl.program_id(0)

    @pl.when(r == 0)
    def _():
        load_pieces(pieces, kv, sem, offsets, counts)
        acc[...] = jnp.zeros(acc.shape, F32)

    i = sc[0] ^ r
    lo = sc[1 + 2 * i]
    hi = sc[2 + 2 * i]
    start = se_ref[0:1, :]
    end = se_ref[1:2, :]
    start = twice(start)
    end = twice(end)
    head_query = by_head(q_ref[...].astype(F32) * SCALE)
    head_grad = by_head(g_ref[0].astype(F32))
    peak = jnp.concatenate([st_ref[0:1, :], st_ref[1:2, :]], axis=1)
    inverse = jnp.concatenate([st_ref[2:3, :], st_ref[3:4, :]], axis=1)

    def first(j, dot8):
        score = scores_of(kv, head_query, j, start, end)
        weight = jnp.exp(score - peak) * inverse
        vals = kv[pl.ds(pl.multiple_of(j * TILE, TILE), TILE), PAIR : 2 * PAIR]
        grad_prob = nt(vals, head_grad)
        w_scr[j - lo] = weight
        g_scr[j - lo] = grad_prob
        return dot8 + fold8(weight * grad_prob, jnp.sum)

    dot8 = lax.fori_loop(lo, hi, first, jnp.zeros((8, 2 * TILE), F32))
    rowdot = jnp.sum(dot8, axis=0, keepdims=True)
    dq_scr[...] = jnp.zeros(dq_scr.shape, F32)

    def second(j, carry):
        weight = w_scr[j - lo]
        grad_score = (weight * (g_scr[j - lo] - rowdot)).astype(BF)
        prob = weight.astype(BF)
        at = pl.ds(pl.multiple_of(j * TILE, TILE), TILE)
        acc[at, 0:PAIR] += nn(grad_score, head_query)
        acc[at, PAIR : 2 * PAIR] += nn(prob, head_grad)
        dq_scr[...] += tn(kv[at, 0:PAIR], grad_score)
        return carry

    lax.fori_loop(lo, hi, second, 0)
    dq_ref[...] = (joined(dq_scr[...]).T * SCALE).astype(BF)

    @pl.when(r == pl.num_programs(0) - 1)
    def _():
        for k in range(n):
            piece = acc[offsets[k] : offsets[k] + counts[k], :]
            outs[k][...] = piece.astype(outs[k].dtype)


def bwd_call(pair, sc, query, spans, stats, grads, pieces, offsets, counts, own):
    rows = query.shape[0]
    near = sum(counts)

    def whole(count):
        return pl.BlockSpec((count, 2 * PAIR), lambda r, sc: (0, 0))

    return pl.pallas_call(
        functools.partial(bwd_kernel, offsets, counts),
        grid_spec=pltpu.PrefetchScalarGridSpec(
            num_scalar_prefetch=1,
            grid=(rows // TILE,),
            in_specs=[
                pl.BlockSpec((TILE, PAIR), lambda r, sc: (sc[0] ^ r, pair)),
                pl.BlockSpec((8, TILE), lambda r, sc: (0, sc[0] ^ r)),
                pl.BlockSpec((8, TILE), lambda r, sc: (0, sc[0] ^ r)),
                pl.BlockSpec((1, TILE, PAIR), lambda r, sc: (r, 0, pair)),
            ]
            + [pl.BlockSpec(memory_space=pl.ANY)] * len(pieces),
            out_specs=[pl.BlockSpec((TILE, PAIR), lambda r, sc: (sc[0] ^ r, 0))]
            + [whole(c) for c in counts],
            scratch_shapes=[
                pltpu.VMEM((near, 2 * PAIR), BF),
                pltpu.VMEM((near // TILE, TILE, 2 * TILE), F32),
                pltpu.VMEM((near // TILE, TILE, 2 * TILE), F32),
                pltpu.VMEM((near, 2 * PAIR), F32),
                pltpu.VMEM((PAIR, 2 * TILE), F32),
                pltpu.SemaphoreType.DMA((len(pieces),)),
            ],
        ),
        out_shape=[jax.ShapeDtypeStruct((rows, PAIR), BF)]
        + [
            jax.ShapeDtypeStruct((c, 2 * PAIR), F32 if k == own else BF)
            for k, c in enumerate(counts)
        ],
        compiler_params=params(),
        name="attn_bwd",
        cost_estimate=costs(22),
    )(sc, query, spans, stats, grads, *pieces)


def whole_spec(shape):
    return pl.BlockSpec(shape, lambda i, sc: (0,) * len(shape))


def proj_kernel(sc, c0, c1, c2, c3, w0, w1, w2, w3, x0, x1, x2, x3, vec, bt_ref, mid_ref, n2_ref):
    t = sc[0]
    fw = x0.shape[1]
    branch = vec[4:5, :] + sum(
        nn(c[...], w[...]) for c, w in ((c0, w0), (c1, w1), (c2, w2), (c3, w3))
    )
    bt_ref[...] = branch
    chunks = unxor([x[...].astype(F32) for x in (x0, x1, x2, x3)], t)
    for a in range(4):
        at = slice(a * fw, (a + 1) * fw)
        mid_ref[:, at] = chunks[a] + vec[5:6, at] * branch[:, at]
    middle = mid_ref[...]
    mean, rstd = stats_of([middle], 4 * fw)
    n2_ref[...] = ((middle - mean) * rstd * vec[2:3, :] + vec[3:4, :]).astype(BF)


def proj_call(sc, contexts, ws, xs, vec):
    rows, fw = contexts[0].shape
    width = ws[0].shape[1]
    tile = rows // 2

    def row(n):
        return pl.BlockSpec((tile, n), lambda i, sc: (i, 0))

    def mine(n):
        return pl.BlockSpec((tile, n), lambda i, sc: (sc[0] * 2 + i, 0))

    return pl.pallas_call(
        proj_kernel,
        grid_spec=pltpu.PrefetchScalarGridSpec(
            num_scalar_prefetch=1,
            grid=(2,),
            in_specs=[row(fw)] * 4
            + [whole_spec(ws[0].shape)] * 4
            + [mine(fw)] * 4
            + [whole_spec(vec.shape)],
            out_specs=[row(width)] * 3,
        ),
        out_shape=[
            jax.ShapeDtypeStruct((rows, width), F32),
            jax.ShapeDtypeStruct((rows, width), F32),
            jax.ShapeDtypeStruct((rows, width), BF),
        ],
        compiler_params=params(),
        name="proj",
        cost_estimate=costs(4),
    )(sc, *contexts, *ws, *xs, vec)


def mlp_kernel(n0, n1, g0, g1, fc1, fc2, bias, h_ref, gb_ref, s0, s1, d0, d1, fb_ref):
    i = pl.program_id(0)
    step = 256
    hidden_units = fc1.shape[0]

    @pl.when(i == 0)
    def _():
        fb_ref[...] = jnp.zeros(fb_ref.shape, F32)

    def work(n_ref, g_ref, s_ref, d_ref):
        normed = n_ref[...]
        grads = g_ref[...]
        for u in range(hidden_units // step):
            at = slice(u * step, (u + 1) * step)
            before = nt(normed, fc1[at, :]) + bias[:, at]
            phi = 0.5 * (1.0 + lax.erf(before * INV_SQRT2))
            h_ref[:, at] = (before * phi).astype(BF)
            slope = phi + before * (jnp.exp(-0.5 * before * before) * INV_SQRT2PI)
            grad_before = (slope * nt(grads, fc2[at, :])).astype(BF)
            gb_ref[:, at] = grad_before
            wide = grad_before.astype(F32)
            fb_ref[0:1, at] += jnp.sum(wide, axis=0, keepdims=True)
        d_ref[...] = nn(gb_ref[...], fc1[...]).astype(BF)
        s_ref[...] = nn(h_ref[...], fc2[...]).astype(BF)

    @pl.when(i == 0)
    def _():
        work(n0, g0, s0, d0)

    @pl.when(i == 1)
    def _():
        work(n1, g1, s1, d1)


def mlp_call(normed, grads, weights, bias):
    rows, width = normed[0].shape
    hidden_units = bias.shape[1]

    def full(shape):
        return pl.BlockSpec(shape, lambda i: (0,) * len(shape))

    piece = jax.ShapeDtypeStruct((rows, width), BF)
    return pl.pallas_call(
        mlp_kernel,
        grid=(2,),
        in_specs=[full((rows, width))] * 4
        + [
            pl.BlockSpec((hidden_units, width), lambda i: (0, 0)),
            pl.BlockSpec((hidden_units, width), lambda i: (1, 0)),
            full(bias.shape),
        ],
        out_specs=[pl.BlockSpec((rows, hidden_units), lambda i: (i, 0))] * 2
        + [full((rows, width))] * 4
        + [full((8, hidden_units))],
        out_shape=[jax.ShapeDtypeStruct((2 * rows, hidden_units), BF)] * 2
        + [piece] * 4
        + [jax.ShapeDtypeStruct((8, hidden_units), F32)],
        compiler_params=params(),
        name="mlp",
        cost_estimate=costs(10),
    )(*normed, *grads, weights, weights, bias)


def wgrad_kernel(n0, n1, n2, n3, g0, g1, g2, g3, ba, bb, ha, hb, out):
    hidden_units = ba.shape[1]
    for k, (lefts, rights) in enumerate((((n0, n1, n2, n3), (ba, bb)), ((g0, g1, g2, g3), (ha, hb)))):
        total = 0.0
        for half in range(2):
            left = jnp.concatenate([lefts[2 * half][...], lefts[2 * half + 1][...]], axis=0)
            total = total + tn(left, rights[half][...])
        out[:, k * hidden_units : (k + 1) * hidden_units] = total.astype(BF)


def wgrad_call(normed, grads, befores, hiddens):
    sub, width = normed[0].shape
    rows, hidden_units = befores[0].shape
    tile = TILE

    def left():
        return pl.BlockSpec((sub, tile), lambda i: (0, i))

    def right():
        return pl.BlockSpec((rows, hidden_units), lambda i: (0, 0))

    return pl.pallas_call(
        wgrad_kernel,
        grid=(width // tile,),
        in_specs=[left()] * 8 + [right()] * 4,
        out_specs=pl.BlockSpec((tile, 2 * hidden_units), lambda i: (i, 0)),
        out_shape=jax.ShapeDtypeStruct((width, 2 * hidden_units), BF),
        compiler_params=params(),
        name="wgrads",
        cost_estimate=costs(9),
    )(*normed, *grads, *befores, *hiddens)


def mid_kernel(
    sc, a0, a1, a2, k0, k1, k2, k3, mid, bt, w0, w1, w2, w3, vec, gm_ref, gb_ref, gc_ref, sums
):
    t = sc[0]
    fw = k0.shape[1]
    width = 4 * fw

    @pl.when(pl.program_id(0) == 0)
    def _():
        sums[...] = jnp.zeros(sums.shape, F32)

    grad_normed = a0[...].astype(F32) + a1[...].astype(F32) + a2[...].astype(F32)
    middle = mid[...]
    mean, rstd = stats_of([middle], width)
    scaled = (middle - mean) * rstd
    inner = grad_normed * vec[2:3, :]
    mean_a = jnp.sum(inner, axis=1, keepdims=True) / width
    mean_b = jnp.sum(inner * scaled, axis=1, keepdims=True) / width
    chunks = unxor([k[...].astype(F32) for k in (k0, k1, k2, k3)], t)
    back = rstd * (inner - mean_a - scaled * mean_b)
    for a in range(4):
        at = slice(a * fw, (a + 1) * fw)
        gm_ref[:, at] = chunks[a] + back[:, at]
    grad_middle = gm_ref[...]
    grad_branch = grad_middle * vec[5:6, :]
    small = grad_branch.astype(BF)
    gb_ref[...] = small
    for r, w in enumerate((w0, w1, w2, w3)):
        gc_ref[r] = nt(small, w[...]).astype(BF)

    def add(k, values):
        sums[k : k + 1, :] += jnp.sum(values, axis=0, keepdims=True)

    add(0, grad_normed * scaled)
    add(1, grad_normed)
    add(2, grad_middle * bt[...])
    add(3, grad_branch)


def mid_call(sc, parts, cots, middle, branch, ws, vec):
    rows, width = middle.shape
    fw = width // 4
    tile = rows // 2

    def row(n):
        return pl.BlockSpec((tile, n), lambda i, sc: (i, 0))

    return pl.pallas_call(
        mid_kernel,
        grid_spec=pltpu.PrefetchScalarGridSpec(
            num_scalar_prefetch=1,
            grid=(2,),
            in_specs=[row(width)] * 3
            + [row(fw)] * 4
            + [row(width)] * 2
            + [whole_spec(ws[0].shape)] * 4
            + [whole_spec(vec.shape)],
            out_specs=[
                row(width),
                row(width),
                pl.BlockSpec((4, tile, fw), lambda i, sc: (0, i, 0)),
                whole_spec((8, width)),
            ],
        ),
        out_shape=[
            jax.ShapeDtypeStruct((rows, width), F32),
            jax.ShapeDtypeStruct((rows, width), BF),
            jax.ShapeDtypeStruct((4, rows, fw), BF),
            jax.ShapeDtypeStruct((8, width), F32),
        ],
        compiler_params=params(),
        name="mid",
        cost_estimate=costs(6),
    )(sc, *parts, *cots, middle, branch, *ws, vec)


def gn1_kernel(sc, gq0, gq1, gk, gv, w_ref, o0, o1, o2, o3):
    width = w_ref.shape[1] // 3
    query = jnp.concatenate([gq0[...], gq1[...]], axis=1)
    total = (
        nn(query, w_ref[:, 0:width])
        + nn(gk[...], w_ref[:, width : 2 * width])
        + nn(gv[...], w_ref[:, 2 * width : 3 * width])
    ).astype(BF)
    for r, ref in enumerate((o0, o1, o2, o3)):

        @pl.when(pl.program_id(0) == r)
        def _():
            ref[...] = total


def gn1_call(sc, gq0, gq1, gk, gv, w):
    rows = gk.shape[0]
    features, wide = w.shape
    sub = rows // 4

    def row(n):
        return pl.BlockSpec((sub, n), lambda r, sc: (sc[0] ^ r, 0))

    return pl.pallas_call(
        gn1_kernel,
        grid_spec=pltpu.PrefetchScalarGridSpec(
            num_scalar_prefetch=1,
            grid=(4,),
            in_specs=[row(PAIR), row(PAIR), row(features), row(features), whole_spec(w.shape)],
            out_specs=[whole_spec((sub, wide // 3))] * 4,
        ),
        out_shape=[jax.ShapeDtypeStruct((sub, wide // 3), BF)] * 4,
        compiler_params=params(),
        name="gn1",
        cost_estimate=costs(6),
    )(sc, gq0, gq1, gk, gv, w)


def qkvg_kernel(gq, gk, gv, n1, out):
    unit = out.shape[2]
    per = n1.shape[1] // unit
    for c, ref in enumerate((gq, gk, gv)):
        both = tn(ref[...], n1[...]).astype(BF)
        for k in range(per):
            out[c * per + k] = both[:, k * unit : (k + 1) * unit]


def qkvg_call(gq, gk, gv, n1):
    features = gq.shape[1]
    unit = n1.shape[1] // 8
    return pl.pallas_call(
        qkvg_kernel,
        out_shape=jax.ShapeDtypeStruct((24, features, unit), BF),
        compiler_params=params(0),
        name="qkv_grad",
        cost_estimate=costs(5),
    )(gq, gk, gv, n1)


def nsum_kernel(sc, a0, a1, a2, a3, x0, x1, x2, x3, sums):
    t = sc[0]
    r = pl.program_id(0)
    width = 4 * x0.shape[1]

    @pl.when(r == 0)
    def _():
        sums[...] = jnp.zeros(sums.shape, F32)

    value = jnp.concatenate(unxor([x[...].astype(F32) for x in (x0, x1, x2, x3)], t), axis=1)
    mean, rstd = stats_of([value], width)
    scaled = (value - mean) * rstd
    for k, ref in enumerate((a0, a1, a2, a3)):

        @pl.when(r == k)
        def _():
            part = ref[...].astype(F32)
            sums[0:1, :] += jnp.sum(part * scaled, axis=0, keepdims=True)
            sums[1:2, :] += jnp.sum(part, axis=0, keepdims=True)


def nsum_call(sc, pieces, xs):
    sub, width = pieces[0].shape
    fw = width // 4
    return pl.pallas_call(
        nsum_kernel,
        grid_spec=pltpu.PrefetchScalarGridSpec(
            num_scalar_prefetch=1,
            grid=(4,),
            in_specs=[whole_spec((sub, width))] * 4
            + [pl.BlockSpec((sub, fw), lambda r, sc: (sc[0] ^ r, 0))] * 4,
            out_specs=whole_spec((8, width)),
        ),
        out_shape=jax.ShapeDtypeStruct((8, width), F32),
        compiler_params=params(),
        name="norm_sums",
        cost_estimate=costs(5),
    )(sc, *pieces, *xs)


def last_kernel(sc, a0, a1, a2, x0, x1, x2, x3, gm, vec, o0, o1, o2, o3, scr):
    t = sc[0]
    fw = x0.shape[1]
    width = 4 * fw

    grad_normed = a0[...].astype(F32) + a1[...].astype(F32) + a2[...].astype(F32)
    chunks = unxor([x[...].astype(F32) for x in (x0, x1, x2, x3)], t)
    value = jnp.concatenate(chunks, axis=1)
    mean, rstd = stats_of([value], width)
    scaled = (value - mean) * rstd
    inner = grad_normed * vec[0:1, :]
    mean_a = jnp.sum(inner, axis=1, keepdims=True) / width
    mean_b = jnp.sum(inner * scaled, axis=1, keepdims=True) / width
    scr[...] = (gm[...] + rstd * (inner - mean_a - scaled * mean_b)).astype(BF)
    for r, ref in enumerate((o0, o1, o2, o3)):
        ref[...] = scr[:, pl.ds(pl.multiple_of((t ^ r) * fw, fw), fw)]


def last_call(sc, parts, xs, grad_middle, vec):
    rows, width = grad_middle.shape
    fw = width // 4
    tile = rows // 2

    def row(n):
        return pl.BlockSpec((tile, n), lambda i, sc: (i, 0))

    def mine(n):
        return pl.BlockSpec((tile, n), lambda i, sc: (sc[0] * 2 + i, 0))

    return pl.pallas_call(
        last_kernel,
        grid_spec=pltpu.PrefetchScalarGridSpec(
            num_scalar_prefetch=1,
            grid=(2,),
            in_specs=[row(width)] * 3 + [mine(fw)] * 4 + [row(width), whole_spec(vec.shape)],
            out_specs=[row(fw)] * 4,
            scratch_shapes=[pltpu.VMEM((tile, width), BF)],
        ),
        out_shape=[jax.ShapeDtypeStruct((rows, fw), BF)] * 4,
        compiler_params=params(),
        name="last",
        cost_estimate=costs(3),
    )(sc, *parts, *xs, grad_middle, vec)


def out_kernel(sc, a0, a1, a2, k0, k1, k2, k3, mid, vec, o0, o1, o2, o3, sums, scr):
    t = sc[0]
    fw = k0.shape[1]

    @pl.when(pl.program_id(0) == 0)
    def _():
        sums[...] = jnp.zeros(sums.shape, F32)

    total = a0[...].astype(F32) + a1[...].astype(F32) + a2[...].astype(F32) + vec[6:7, :]
    scr[...] = (mid[...] + vec[7:8, :] * total).astype(BF)
    for r, ref in enumerate((o0, o1, o2, o3)):
        ref[...] = scr[:, pl.ds(pl.multiple_of((t ^ r) * fw, fw), fw)]
    grad = jnp.concatenate(unxor([k[...].astype(F32) for k in (k0, k1, k2, k3)], t), axis=1)
    sums[0:1, :] += jnp.sum(grad * total, axis=0, keepdims=True)
    sums[1:2, :] += jnp.sum(grad * vec[7:8, :], axis=0, keepdims=True)


def out_call(sc, parts, cots, middle, vec):
    rows, width = middle.shape
    fw = width // 4
    tile = rows // 2

    def row(n):
        return pl.BlockSpec((tile, n), lambda i, sc: (i, 0))

    return pl.pallas_call(
        out_kernel,
        grid_spec=pltpu.PrefetchScalarGridSpec(
            num_scalar_prefetch=1,
            grid=(2,),
            in_specs=[row(width)] * 3 + [row(fw)] * 4 + [row(width), whole_spec(vec.shape)],
            out_specs=[row(fw)] * 4 + [whole_spec((8, width))],
            scratch_shapes=[pltpu.VMEM((tile, width), BF)],
        ),
        out_shape=[jax.ShapeDtypeStruct((rows, fw), BF)] * 4
        + [jax.ShapeDtypeStruct((8, width), F32)],
        compiler_params=params(),
        name="block_out",
        cost_estimate=costs(3),
    )(sc, *parts, *cots, middle, vec)


def after(*values):
    return lax.optimization_barrier(values)


def placed(pieces, t, axis):
    return jnp.concatenate(unxor(pieces, t), axis=axis)


def reduce4(pieces):
    far = (pieces[2].astype(F32) + px(pieces[3], 1).astype(F32)).astype(BF)
    return pieces[0], px(pieces[1], 1), px(far, 2)


def halved(blocks, s):
    for axis, bits, place in ((1, 2, 1), (1, 1, 0), (0, 4, 2)):
        mine = (s >> place) & 1
        keep = lax.dynamic_index_in_dim(blocks, mine, axis, keepdims=False)
        send = lax.dynamic_index_in_dim(blocks, 1 - mine, axis, keepdims=False)
        got = ps(send.astype(BF), bits)
        blocks = keep.astype(F32) + got.astype(F32)
    return blocks


def spans_of(image_ids, row_count, first_row, margin, near):
    tokens = image_ids.shape[0]
    most = tokens // IMG_LEAST + 1
    place = jnp.arange(tokens, dtype=jnp.int32)
    names = jnp.arange(most, dtype=jnp.int32)[:, None]
    same = image_ids[None, :] == names
    low = jnp.min(jnp.where(same, place[None, :], tokens), axis=1)
    high = jnp.max(jnp.where(same, place[None, :] + 1, 0), axis=1)
    own = lax.dynamic_slice_in_dim(image_ids, first_row, row_count, 0)
    mine = own[None, :] == names
    start = jnp.sum(jnp.where(mine, low[:, None], 0), axis=0)
    end = jnp.sum(jnp.where(mine, high[:, None], 0), axis=0)
    valid = own >= 0
    shift = margin - first_row
    start = jnp.where(valid, start + shift, 0)
    end = jnp.where(valid, end + shift, 0)
    lo = jnp.min(jnp.where(valid, start, near).reshape(-1, TILE), axis=1)
    hi = jnp.max(end.reshape(-1, TILE), axis=1)
    lo = jnp.clip(lo // TILE, 0, near // TILE)
    hi = jnp.clip(-(-hi // TILE), 0, near // TILE)
    spans = jnp.concatenate(
        [start[None, :], end[None, :], jnp.zeros((6, row_count), jnp.int32)], axis=0
    )
    return spans, jnp.stack([lo, hi], axis=1).reshape(-1)


def per_device(
    block_input,
    cotangent,
    image_ids,
    qkv_weight,
    proj_weight,
    fc1_weight,
    fc2_weight,
    norm1_gain,
    norm1_shift,
    q_bias,
    v_bias,
    proj_bias,
    scale_attn,
    norm2_gain,
    norm2_shift,
    fc1_bias,
    fc2_bias,
    scale_mlp,
):
    row_count, fw = block_input.shape
    n_seq = lax.axis_size("seq")
    width = 4 * fw
    features = qkv_weight.shape[0]
    sub = row_count // 4
    t = lax.axis_index("tensor").astype(jnp.int32)
    s = lax.axis_index("seq").astype(jnp.int32)
    reach = (IMG - 1 + row_count - 1) // row_count
    tile_rows = min(128, row_count)

    xs = gather4(block_input)
    if n_seq == 8:
        own = jnp.concatenate([qkv_weight, proj_weight], axis=1)
        z2, z4, z6 = ps(own, 2), ps(own, 4), ps(own, 6)
        found = [None] * 8
        for bits, piece in ((0, own), (2, z2), (4, z4), (6, z6)):
            found[bits] = piece
            found[bits ^ 1] = ps(piece, 1)
        w_qkv = jnp.zeros((8,) + own.shape, BF)
        for bits in range(8):
            w_qkv = lax.dynamic_update_slice(w_qkv, found[bits][None], (s ^ bits, 0, 0))
    else:
        w_qkv = jnp.concatenate(
            [
                lax.all_gather(w, "seq", axis=1, tiled=True)[None]
                for w in (qkv_weight, proj_weight)
            ],
            axis=2,
        )
    vec_own = jnp.stack(
        [
            norm1_gain,
            norm1_shift,
            norm2_gain,
            norm2_shift,
            proj_bias,
            scale_attn,
            fc2_bias,
            scale_mlp,
        ]
    )
    vec = placed([vec_own] + [px(vec_own, r) for r in range(1, 4)], t, 1)
    units = fc1_weight.shape[0]

    offsets_of = []
    counts = []
    for place in range(2 * reach + 1):
        offset = reach - place
        if offset == 0:
            count = row_count
        else:
            need = IMG - 1 - (abs(offset) - 1) * row_count
            count = min(row_count, -(-need // tile_rows) * tile_rows)
        offsets_of.append(offset)
        counts.append(count)
    offsets = [sum(counts[:k]) for k in range(len(counts))]
    near = sum(counts)
    margin = offsets[reach]
    spans, edges = spans_of(image_ids, row_count, s * row_count, margin, near)
    sc = jnp.concatenate([t[None], edges])
    sc_t = t[None]

    normed1, query, kv0, kv1, w_full, proj_full = qkv_call(
        sc_t, xs, w_qkv, vec, q_bias[None, :], v_bias[None, :]
    )
    nears = []
    for kv in (kv0, kv1):
        pieces = []
        for offset, count in zip(offsets_of, counts):
            if offset == 0:
                pieces.append(kv)
            elif offset > 0:
                pieces.append(passed_along(kv[row_count - count :], offset))
            else:
                pieces.append(passed_along(kv[:count], offset))
        nears.append(pieces)
    cots = swap4([rows_at(cotangent, t ^ r, sub) for r in range(4)])
    grad_second = (
        jnp.concatenate(unxor(cots, t), axis=1).astype(F32) * vec[7:8, :]
    ).astype(BF)
    grads = gather4(grad_second)
    contexts = []
    stats = []
    stacked = jnp.concatenate([fc1_weight, fc2_weight], axis=0)
    stacked, *nears[0] = after(stacked, *nears[0])
    others = lax.all_gather(stacked, "seq", axis=1, tiled=True)
    ws = gather4(proj_full)
    for pair in range(2):
        ctx, st = fwd_call(pair, sc, query, spans, nears[pair], offsets, counts)
        if pair == 0:
            ctx, *rest = after(ctx, *ws, *grads)
            ws, grads = rest[:4], rest[4:]
        contexts.append(ctx)
        stats.append(st)
    context = jnp.concatenate(contexts, axis=1)
    ctx_rows = swap4([rows_at(context, t ^ r, sub) for r in range(4)])
    branch, middle, normed2 = proj_call(sc_t, ctx_rows, ws, xs, vec)
    n_near = px(normed2, 1)
    n_across = px(normed2, 2)
    n_far = px(n_across, 1)
    bias1 = fc1_bias[None, :]
    hid_b, gb_b, s2, s3, d2, d3, fb_b = mlp_call((n_across, n_far), grads[2:], others, bias1)
    far = (d2.astype(F32) + px(d3, 1).astype(F32)).astype(BF)
    far, n_near = after(far, n_near)
    far = px(far, 2)
    hid_a, gb_a, s0, s1, d0, d1, fb_a = mlp_call((normed2, n_near), grads[:2], others, bias1)
    from_near = px(d1, 1)

    fc_part = wgrad_call((normed2, n_near, n_across, n_far), grads, (gb_a, gb_b), (hid_a, hid_b))
    far, fc_part = after(far, fc_part)
    fc_out = lax.psum_scatter(fc_part, "seq", scatter_dimension=0, tiled=True)
    grad_middle, grad_branch, grad_ctx, sums_mid = mid_call(
        sc_t, (d0, from_near, far), cots, middle, branch, ws, vec
    )
    grad_rows = jnp.stack(swap4([grad_ctx[r] for r in range(4)]))
    grad_rows, grad_branch, s0, s1, s2, s3 = after(grad_rows, grad_branch, s0, s1, s2, s3)
    seconds = reduce4([s0, s1, s2, s3])
    branch_all = gather4(grad_branch)

    grad_q = []
    grad_k = []
    grad_v = []
    for pair in range(2):
        got = bwd_call(
            pair, sc, query, spans, stats[pair], grad_rows, nears[pair], offsets, counts, reach
        )
        got = list(got)
        if pair == 0:
            got[1], grad_rows = after(got[1], grad_rows)
        if pair == 0:
            got[0], *branch_all = after(got[0], *branch_all)
            branch_rows = placed(branch_all, t, 0)
            proj_part = tn(branch_rows, context).astype(BF)
            if n_seq == 8:
                proj_out = halved(proj_part.reshape(2, 2, 2, width // 8, features), s)
            else:
                proj_out = lax.psum_scatter(proj_part, "seq", scatter_dimension=0, tiled=True)
        else:
            got[0], *seconds = after(got[0], *seconds)
            o0, o1, o2, o3, sums_out = out_call(sc_t, seconds, cots, middle, vec)
            block_output = placed(swap4([o0, o1, o2, o3]), t, 0)
        grad_q.append(got[0])
        total = got[1 + reach]
        for k, (offset, count) in enumerate(zip(offsets_of, counts)):
            if offset == 0:
                continue
            back = passed_along(got[1 + k], -offset).astype(F32)
            if count < row_count:
                gap = row_count - count
                ends = ((gap, 0), (0, 0)) if offset > 0 else ((0, gap), (0, 0))
                back = jnp.pad(back, ends)
            total = total + back
        total = total.astype(BF)
        grad_k.append(total[:, :PAIR])
        grad_v.append(total[:, PAIR:])
    gk = jnp.concatenate(grad_k, axis=1)
    gv = jnp.concatenate(grad_v, axis=1)
    gq = jnp.concatenate(grad_q, axis=1)
    if n_seq == 8:
        unit = width // 8
        blocks = qkvg_call(gq, gk, gv, normed1).reshape(2, 2, 2, 3, features, unit)
        blocks, gk = after(blocks, gk)
        blocks = halved(blocks, s)
        qkv_out = jnp.concatenate([blocks[k] for k in range(3)], axis=1)
    else:
        qkv_parts = [tn(g, normed1) for g in (gq, gk, gv)]
        qkv_out = lax.psum_scatter(
            jnp.stack(qkv_parts, axis=1).reshape(features, 3 * width).astype(BF),
            "seq",
            scatter_dimension=1,
            tiled=True,
        ).astype(F32)
    pieces = gn1_call(sc_t, grad_q[0], grad_q[1], gk, gv, w_full)
    sums_last = nsum_call(sc_t, pieces, xs)
    i0, i1, i2, i3 = last_call(sc_t, reduce4(pieces), xs, grad_middle, vec)
    input_grad = placed(swap4([i0, i1, i2, i3]), t, 0)

    rows8 = jnp.concatenate([sums_last[0:2], sums_mid[0:4], sums_out[0:2]], axis=0)
    cut = [lax.dynamic_slice_in_dim(rows8, (t ^ r) * fw, fw, 1) for r in range(4)]
    got = swap4(cut)
    own8 = got[0] + got[1] + got[2] + got[3]
    flat = jnp.concatenate(
        [
            own8.reshape(-1),
            jnp.sum(gq.astype(F32), axis=0),
            jnp.sum(gv.astype(F32), axis=0),
            fb_a[0] + fb_b[0],
        ]
    ).reshape(-1, 128)
    if n_seq == 8:
        for bits in (2, 1, 4):
            flat = flat + ps(flat, bits)
    else:
        flat = lax.psum(flat, "seq")
    flat = flat.reshape(-1)
    own8 = flat[: 8 * fw].reshape(8, fw)
    q_bias_grad = flat[8 * fw : 8 * fw + features]
    v_bias_grad = flat[8 * fw + features : 8 * fw + 2 * features]
    fc1_bias_grad = flat[8 * fw + 2 * features :]
    return (
        block_output,
        input_grad,
        qkv_out,
        proj_out.T.astype(F32),
        fc_out[:, :units].T.astype(F32),
        fc_out[:, units:].T.astype(F32),
        own8[0],
        own8[1],
        q_bias_grad,
        v_bias_grad,
        own8[5],
        own8[4],
        own8[2],
        own8[3],
        fc1_bias_grad,
        own8[7],
        own8[6],
    )


def solution(mesh):
    cut = P("tensor", "seq")
    by_tensor = P("tensor")
    in_specs = (P("seq", "tensor"), P("seq", "tensor"), P()) + (cut,) * 4 + (by_tensor,) * 11
    out_specs = (P("seq", "tensor"), P("seq", "tensor")) + (cut,) * 4 + (by_tensor,) * 11

    return jax.shard_map(
        per_device, mesh=mesh, in_specs=in_specs, out_specs=out_specs, check_vma=False
    )
```

```python
import functools

import jax
import jax.numpy as jnp
from jax import lax
from jax.experimental import pallas as pl
from jax.experimental.pallas import tpu as pltpu
from jax.sharding import PartitionSpec as P


HEAD_DIM = 64
IMG = 1370
IMG_LEAST = 686
EPS = 1e-06
NEG = -1e30
BF = jnp.bfloat16
F32 = jnp.float32
TILE = 256
PAIR = 2 * HEAD_DIM
SCALE = HEAD_DIM ** (-0.5)
INV_SQRT2 = 0.7071067811865476
INV_SQRT2PI = 0.3989422804014327


def px(value, bits):
    pairs = [(i, i ^ bits) for i in range(lax.axis_size("tensor"))]
    return lax.ppermute(value, "tensor", pairs)


def ps(value, bits):
    pairs = [(i, i ^ bits) for i in range(lax.axis_size("seq"))]
    return lax.ppermute(value, "seq", pairs)


def passed_along(block, distance):
    devices = range(lax.axis_size("seq"))
    route = [(i - distance, i) for i in devices if i - distance in devices]
    return lax.ppermute(block, "seq", route)


def gather4(value):
    across = px(value, 2)
    return [value, px(value, 1), across, px(across, 1)]


def swap4(pieces):
    return [pieces[0]] + [px(pieces[r], r) for r in range(1, 4)]


def rows_at(value, index, size):
    return lax.dynamic_slice_in_dim(value, index * size, size, 0)


def unxor(pieces, t):
    low = (t & 1) == 1
    high = (t & 2) == 2
    first = [jnp.where(low, pieces[r ^ 1], pieces[r]) for r in range(4)]
    return [jnp.where(high, first[r ^ 2], first[r]) for r in range(4)]


def nt(left, right):
    return lax.dot_general(left, right, (((1,), (1,)), ((), ())), preferred_element_type=F32)


def nn(left, right):
    return lax.dot_general(left, right, (((1,), (0,)), ((), ())), preferred_element_type=F32)


def tn(left, right):
    return lax.dot_general(left, right, (((0,), (0,)), ((), ())), preferred_element_type=F32)


def params(n=1, limit=56):
    return pltpu.CompilerParams(
        dimension_semantics=("arbitrary",) * n, vmem_limit_bytes=limit * 1024 * 1024
    )


def costs(micros):
    return pl.CostEstimate(flops=int(micros * 1e9), transcendentals=0, bytes_accessed=1 << 20)


def stats_of(chunks, width):
    total = sum(jnp.sum(c, axis=1, keepdims=True) for c in chunks)
    square = sum(jnp.sum(c * c, axis=1, keepdims=True) for c in chunks)
    mean = total / width
    rstd = lax.rsqrt(square / width - mean * mean + EPS)
    return mean, rstd


def qkv_kernel(sc, x0, x1, x2, x3, w_ref, vec, qb, vb, n1_ref, q_ref, kv0_ref, kv1_ref, wout, wproj, wscr):
    groups = w_ref.shape[0]
    part = w_ref.shape[2] * 3 // 4
    small = w_ref.shape[2] - part

    @pl.when(pl.program_id(0) == 0)
    def _():
        for g in range(groups):
            wscr[:, g * part : (g + 1) * part] = w_ref[g, :, :part]
            wproj[:, g * small : (g + 1) * small] = w_ref[g, :, part:]
        wout[...] = wscr[...]

    t = sc[0]
    chunks = unxor([r[...].astype(F32) for r in (x0, x1, x2, x3)], t)
    fw = x0.shape[1]
    width = 4 * fw
    mean, rstd = stats_of(chunks, width)
    for a in range(4):
        lo = a * fw
        scaled = (chunks[a] - mean) * rstd
        n1_ref[:, lo : lo + fw] = (
            scaled * vec[0:1, lo : lo + fw] + vec[1:2, lo : lo + fw]
        ).astype(BF)
    normed = n1_ref[...]
    query = nt(normed, wscr[:, 0:width]) + qb[...]
    q_ref[...] = query.astype(BF)
    key = nt(normed, wscr[:, width : 2 * width]).astype(BF)
    value = (nt(normed, wscr[:, 2 * width : 3 * width]) + vb[...]).astype(BF)
    for p, ref in enumerate((kv0_ref, kv1_ref)):
        ref[:, 0:PAIR] = key[:, p * PAIR : (p + 1) * PAIR]
        ref[:, PAIR : 2 * PAIR] = value[:, p * PAIR : (p + 1) * PAIR]


def qkv_call(sc, xs, w, vec, qb, vb):
    rows, fw = xs[0].shape
    groups, features, part = w.shape
    part = part * 3 // 4
    width = 4 * fw
    tile = TILE

    def full(shape):
        return pl.BlockSpec(shape, lambda i, sc: (0,) * len(shape))

    def row(n):
        return pl.BlockSpec((tile, n), lambda i, sc: (i, 0))

    return pl.pallas_call(
        qkv_kernel,
        grid_spec=pltpu.PrefetchScalarGridSpec(
            num_scalar_prefetch=1,
            grid=(rows // tile,),
            in_specs=[row(fw)] * 4
            + [full(w.shape), full(vec.shape), full(qb.shape), full(vb.shape)],
            out_specs=[
                row(width),
                row(features),
                row(2 * PAIR),
                row(2 * PAIR),
                full((features, groups * part)),
                full((features, width)),
            ],
            scratch_shapes=[pltpu.VMEM((features, groups * part), BF)],
        ),
        out_shape=[
            jax.ShapeDtypeStruct((rows, width), BF),
            jax.ShapeDtypeStruct((rows, features), BF),
            jax.ShapeDtypeStruct((rows, 2 * PAIR), BF),
            jax.ShapeDtypeStruct((rows, 2 * PAIR), BF),
            jax.ShapeDtypeStruct((features, groups * part), BF),
            jax.ShapeDtypeStruct((features, width), BF),
        ],
        compiler_params=params(),
        name="qkv",
        cost_estimate=costs(7),
    )(sc, *xs, w, vec, qb, vb)


def load_pieces(pieces, target, sem, offsets, counts):
    copies = [
        pltpu.make_async_copy(ref, target.at[pl.ds(offset, count), :], sem.at[k])
        for k, (ref, offset, count) in enumerate(zip(pieces, offsets, counts))
    ]
    for copy in copies:
        copy.start()
    for copy in copies:
        copy.wait()


def by_head(values):
    lane = lax.broadcasted_iota(jnp.int32, values.shape, 1)
    first = jnp.where(lane < HEAD_DIM, values, 0.0)
    second = jnp.where(lane < HEAD_DIM, 0.0, values)
    return jnp.concatenate([first, second], axis=0).astype(BF)


def joined(values):
    return jnp.concatenate([values[0:HEAD_DIM, :TILE], values[HEAD_DIM:PAIR, TILE:]], axis=0)


def scores_of(kv, head_query, j, start, end):
    raw = nt(kv[pl.ds(pl.multiple_of(j * TILE, TILE), TILE), 0:PAIR], head_query)
    place = lax.broadcasted_iota(jnp.int32, raw.shape, 0) + j * TILE
    return jnp.where((place >= start) & (place < end), raw, NEG)


def fold8(values, how):
    return how(values.reshape(values.shape[0] // 8, 8, values.shape[1]), axis=0)


def twice(row):
    return jnp.concatenate([row, row], axis=1)


def fwd_kernel(offsets, counts, sc, q_ref, se_ref, *refs):
    n = len(counts)
    pieces = refs[:n]
    ctx_ref, st_ref, kv, s_scr, acc, sem = refs[n:]
    i = pl.program_id(0)

    @pl.when(i == 0)
    def _():
        load_pieces(pieces, kv, sem, offsets, counts)

    lo = sc[1 + 2 * i]
    hi = sc[2 + 2 * i]
    start = twice(se_ref[0:1, :])
    end = twice(se_ref[1:2, :])
    head_query = by_head(q_ref[...].astype(F32) * SCALE)

    def first(j, peak):
        score = scores_of(kv, head_query, j, start, end)
        s_scr[j - lo] = score
        return jnp.maximum(peak, fold8(score, jnp.max))

    peak8 = lax.fori_loop(lo, hi, first, jnp.full((8, 2 * TILE), NEG, F32))
    peak = jnp.max(peak8, axis=0, keepdims=True)
    peak = jnp.maximum(peak, 0.1 * NEG)

    def second(j, total):
        expon = jnp.exp(s_scr[j - lo] - peak)
        s_scr[j - lo] = expon
        return total + fold8(expon, jnp.sum)

    total8 = lax.fori_loop(lo, hi, second, jnp.zeros((8, 2 * TILE), F32))
    total = jnp.sum(total8, axis=0, keepdims=True)
    inverse = 1.0 / jnp.where(end > start, total, 1.0)
    acc[...] = jnp.zeros(acc.shape, F32)

    def third(j, carry):
        prob = (s_scr[j - lo] * inverse).astype(BF)
        vals = kv[pl.ds(pl.multiple_of(j * TILE, TILE), TILE), PAIR : 2 * PAIR]
        acc[...] += tn(vals, prob)
        return carry

    lax.fori_loop(lo, hi, third, 0)
    for head in range(2):
        at = slice(head * TILE, (head + 1) * TILE)
        st_ref[head : head + 1, :] = peak[:, at]
        st_ref[2 + head : 3 + head, :] = inverse[:, at]
    ctx_ref[...] = joined(acc[...]).T.astype(BF)


def fwd_call(pair, sc, query, spans, pieces, offsets, counts):
    rows = query.shape[0]
    near = sum(counts)
    return pl.pallas_call(
        functools.partial(fwd_kernel, offsets, counts),
        grid_spec=pltpu.PrefetchScalarGridSpec(
            num_scalar_prefetch=1,
            grid=(rows // TILE,),
            in_specs=[
                pl.BlockSpec((TILE, PAIR), lambda i, sc: (i, pair)),
                pl.BlockSpec((8, TILE), lambda i, sc: (0, i)),
            ]
            + [pl.BlockSpec(memory_space=pl.ANY)] * len(pieces),
            out_specs=[
                pl.BlockSpec((TILE, PAIR), lambda i, sc: (i, 0)),
                pl.BlockSpec((8, TILE), lambda i, sc: (0, i)),
            ],
            scratch_shapes=[
                pltpu.VMEM((near, 2 * PAIR), BF),
                pltpu.VMEM((near // TILE, TILE, 2 * TILE), F32),
                pltpu.VMEM((PAIR, 2 * TILE), F32),
                pltpu.SemaphoreType.DMA((len(pieces),)),
            ],
        ),
        out_shape=[
            jax.ShapeDtypeStruct((rows, PAIR), BF),
            jax.ShapeDtypeStruct((8, rows), F32),
        ],
        compiler_params=params(),
        name="attn_fwd",
        cost_estimate=costs(17),
    )(sc, query, spans, *pieces)


def bwd_kernel(offsets, counts, sc, q_ref, se_ref, st_ref, g_ref, *refs):
    n = len(counts)
    pieces = refs[:n]
    dq_ref = refs[n]
    outs = refs[n + 1 : 2 * n + 1]
    kv, w_scr, g_scr, acc, dq_scr, sem = refs[2 * n + 1 :]
    r = pl.program_id(0)

    @pl.when(r == 0)
    def _():
        load_pieces(pieces, kv, sem, offsets, counts)
        acc[...] = jnp.zeros(acc.shape, F32)

    i = sc[0] ^ r
    lo = sc[1 + 2 * i]
    hi = sc[2 + 2 * i]
    start = se_ref[0:1, :]
    end = se_ref[1:2, :]
    start = twice(start)
    end = twice(end)
    head_query = by_head(q_ref[...].astype(F32) * SCALE)
    head_grad = by_head(g_ref[0].astype(F32))
    peak = jnp.concatenate([st_ref[0:1, :], st_ref[1:2, :]], axis=1)
    inverse = jnp.concatenate([st_ref[2:3, :], st_ref[3:4, :]], axis=1)

    def first(j, dot8):
        score = scores_of(kv, head_query, j, start, end)
        weight = jnp.exp(score - peak) * inverse
        vals = kv[pl.ds(pl.multiple_of(j * TILE, TILE), TILE), PAIR : 2 * PAIR]
        grad_prob = nt(vals, head_grad)
        w_scr[j - lo] = weight
        g_scr[j - lo] = grad_prob
        return dot8 + fold8(weight * grad_prob, jnp.sum)

    dot8 = lax.fori_loop(lo, hi, first, jnp.zeros((8, 2 * TILE), F32))
    rowdot = jnp.sum(dot8, axis=0, keepdims=True)
    dq_scr[...] = jnp.zeros(dq_scr.shape, F32)

    def second(j, carry):
        weight = w_scr[j - lo]
        grad_score = (weight * (g_scr[j - lo] - rowdot)).astype(BF)
        prob = weight.astype(BF)
        at = pl.ds(pl.multiple_of(j * TILE, TILE), TILE)
        acc[at, 0:PAIR] += nn(grad_score, head_query)
        acc[at, PAIR : 2 * PAIR] += nn(prob, head_grad)
        dq_scr[...] += tn(kv[at, 0:PAIR], grad_score)
        return carry

    lax.fori_loop(lo, hi, second, 0)
    dq_ref[...] = (joined(dq_scr[...]).T * SCALE).astype(BF)

    @pl.when(r == pl.num_programs(0) - 1)
    def _():
        for k in range(n):
            piece = acc[offsets[k] : offsets[k] + counts[k], :]
            outs[k][...] = piece.astype(outs[k].dtype)


def bwd_call(pair, sc, query, spans, stats, grads, pieces, offsets, counts, own):
    rows = query.shape[0]
    near = sum(counts)

    def whole(count):
        return pl.BlockSpec((count, 2 * PAIR), lambda r, sc: (0, 0))

    return pl.pallas_call(
        functools.partial(bwd_kernel, offsets, counts),
        grid_spec=pltpu.PrefetchScalarGridSpec(
            num_scalar_prefetch=1,
            grid=(rows // TILE,),
            in_specs=[
                pl.BlockSpec((TILE, PAIR), lambda r, sc: (sc[0] ^ r, pair)),
                pl.BlockSpec((8, TILE), lambda r, sc: (0, sc[0] ^ r)),
                pl.BlockSpec((8, TILE), lambda r, sc: (0, sc[0] ^ r)),
                pl.BlockSpec((1, TILE, PAIR), lambda r, sc: (r, 0, pair)),
            ]
            + [pl.BlockSpec(memory_space=pl.ANY)] * len(pieces),
            out_specs=[pl.BlockSpec((TILE, PAIR), lambda r, sc: (sc[0] ^ r, 0))]
            + [whole(c) for c in counts],
            scratch_shapes=[
                pltpu.VMEM((near, 2 * PAIR), BF),
                pltpu.VMEM((near // TILE, TILE, 2 * TILE), F32),
                pltpu.VMEM((near // TILE, TILE, 2 * TILE), F32),
                pltpu.VMEM((near, 2 * PAIR), F32),
                pltpu.VMEM((PAIR, 2 * TILE), F32),
                pltpu.SemaphoreType.DMA((len(pieces),)),
            ],
        ),
        out_shape=[jax.ShapeDtypeStruct((rows, PAIR), BF)]
        + [
            jax.ShapeDtypeStruct((c, 2 * PAIR), F32 if k == own else BF)
            for k, c in enumerate(counts)
        ],
        compiler_params=params(),
        name="attn_bwd",
        cost_estimate=costs(22),
    )(sc, query, spans, stats, grads, *pieces)


def whole_spec(shape):
    return pl.BlockSpec(shape, lambda i, sc: (0,) * len(shape))


def proj_kernel(sc, c0, c1, c2, c3, w0, w1, w2, w3, x0, x1, x2, x3, vec, bt_ref, mid_ref, n2_ref):
    t = sc[0]
    fw = x0.shape[1]
    branch = vec[4:5, :] + sum(
        nn(c[...], w[...]) for c, w in ((c0, w0), (c1, w1), (c2, w2), (c3, w3))
    )
    bt_ref[...] = branch
    chunks = unxor([x[...].astype(F32) for x in (x0, x1, x2, x3)], t)
    for a in range(4):
        at = slice(a * fw, (a + 1) * fw)
        mid_ref[:, at] = chunks[a] + vec[5:6, at] * branch[:, at]
    middle = mid_ref[...]
    mean, rstd = stats_of([middle], 4 * fw)
    n2_ref[...] = ((middle - mean) * rstd * vec[2:3, :] + vec[3:4, :]).astype(BF)


def proj_call(sc, contexts, ws, xs, vec):
    rows, fw = contexts[0].shape
    width = ws[0].shape[1]
    tile = rows // 2

    def row(n):
        return pl.BlockSpec((tile, n), lambda i, sc: (i, 0))

    def mine(n):
        return pl.BlockSpec((tile, n), lambda i, sc: (sc[0] * 2 + i, 0))

    return pl.pallas_call(
        proj_kernel,
        grid_spec=pltpu.PrefetchScalarGridSpec(
            num_scalar_prefetch=1,
            grid=(2,),
            in_specs=[row(fw)] * 4
            + [whole_spec(ws[0].shape)] * 4
            + [mine(fw)] * 4
            + [whole_spec(vec.shape)],
            out_specs=[row(width)] * 3,
        ),
        out_shape=[
            jax.ShapeDtypeStruct((rows, width), F32),
            jax.ShapeDtypeStruct((rows, width), F32),
            jax.ShapeDtypeStruct((rows, width), BF),
        ],
        compiler_params=params(),
        name="proj",
        cost_estimate=costs(4),
    )(sc, *contexts, *ws, *xs, vec)


def mlp_kernel(n0, n1, g0, g1, fc1, fc2, bias, h_ref, gb_ref, s0, s1, d0, d1, fb_ref):
    i = pl.program_id(0)
    step = 256
    hidden_units = fc1.shape[0]

    @pl.when(i == 0)
    def _():
        fb_ref[...] = jnp.zeros(fb_ref.shape, F32)

    def work(n_ref, g_ref, s_ref, d_ref):
        normed = n_ref[...]
        grads = g_ref[...]
        for u in range(hidden_units // step):
            at = slice(u * step, (u + 1) * step)
            before = nt(normed, fc1[at, :]) + bias[:, at]
            phi = 0.5 * (1.0 + lax.erf(before * INV_SQRT2))
            h_ref[:, at] = (before * phi).astype(BF)
            slope = phi + before * (jnp.exp(-0.5 * before * before) * INV_SQRT2PI)
            grad_before = (slope * nt(grads, fc2[at, :])).astype(BF)
            gb_ref[:, at] = grad_before
            wide = grad_before.astype(F32)
            fb_ref[0:1, at] += jnp.sum(wide, axis=0, keepdims=True)
        d_ref[...] = nn(gb_ref[...], fc1[...]).astype(BF)
        s_ref[...] = nn(h_ref[...], fc2[...]).astype(BF)

    @pl.when(i == 0)
    def _():
        work(n0, g0, s0, d0)

    @pl.when(i == 1)
    def _():
        work(n1, g1, s1, d1)


def mlp_call(normed, grads, weights, bias):
    rows, width = normed[0].shape
    hidden_units = bias.shape[1]

    def full(shape):
        return pl.BlockSpec(shape, lambda i: (0,) * len(shape))

    piece = jax.ShapeDtypeStruct((rows, width), BF)
    return pl.pallas_call(
        mlp_kernel,
        grid=(2,),
        in_specs=[full((rows, width))] * 4
        + [
            pl.BlockSpec((hidden_units, width), lambda i: (0, 0)),
            pl.BlockSpec((hidden_units, width), lambda i: (1, 0)),
            full(bias.shape),
        ],
        out_specs=[pl.BlockSpec((rows, hidden_units), lambda i: (i, 0))] * 2
        + [full((rows, width))] * 4
        + [full((8, hidden_units))],
        out_shape=[jax.ShapeDtypeStruct((2 * rows, hidden_units), BF)] * 2
        + [piece] * 4
        + [jax.ShapeDtypeStruct((8, hidden_units), F32)],
        compiler_params=params(),
        name="mlp",
        cost_estimate=costs(10),
    )(*normed, *grads, weights, weights, bias)


def wgrad_kernel(n0, n1, n2, n3, g0, g1, g2, g3, ba, bb, ha, hb, out):
    hidden_units = ba.shape[1]
    for k, (lefts, rights) in enumerate((((n0, n1, n2, n3), (ba, bb)), ((g0, g1, g2, g3), (ha, hb)))):
        total = 0.0
        for half in range(2):
            left = jnp.concatenate([lefts[2 * half][...], lefts[2 * half + 1][...]], axis=0)
            total = total + tn(left, rights[half][...])
        out[:, k * hidden_units : (k + 1) * hidden_units] = total.astype(BF)


def wgrad_call(normed, grads, befores, hiddens):
    sub, width = normed[0].shape
    rows, hidden_units = befores[0].shape
    tile = TILE

    def left():
        return pl.BlockSpec((sub, tile), lambda i: (0, i))

    def right():
        return pl.BlockSpec((rows, hidden_units), lambda i: (0, 0))

    return pl.pallas_call(
        wgrad_kernel,
        grid=(width // tile,),
        in_specs=[left()] * 8 + [right()] * 4,
        out_specs=pl.BlockSpec((tile, 2 * hidden_units), lambda i: (i, 0)),
        out_shape=jax.ShapeDtypeStruct((width, 2 * hidden_units), BF),
        compiler_params=params(),
        name="wgrads",
        cost_estimate=costs(9),
    )(*normed, *grads, *befores, *hiddens)


def mid_kernel(
    sc, a0, a1, a2, k0, k1, k2, k3, mid, bt, w0, w1, w2, w3, vec, gm_ref, gb_ref, gc_ref, sums
):
    t = sc[0]
    fw = k0.shape[1]
    width = 4 * fw

    @pl.when(pl.program_id(0) == 0)
    def _():
        sums[...] = jnp.zeros(sums.shape, F32)

    grad_normed = a0[...].astype(F32) + a1[...].astype(F32) + a2[...].astype(F32)
    middle = mid[...]
    mean, rstd = stats_of([middle], width)
    scaled = (middle - mean) * rstd
    inner = grad_normed * vec[2:3, :]
    mean_a = jnp.sum(inner, axis=1, keepdims=True) / width
    mean_b = jnp.sum(inner * scaled, axis=1, keepdims=True) / width
    chunks = unxor([k[...].astype(F32) for k in (k0, k1, k2, k3)], t)
    back = rstd * (inner - mean_a - scaled * mean_b)
    for a in range(4):
        at = slice(a * fw, (a + 1) * fw)
        gm_ref[:, at] = chunks[a] + back[:, at]
    grad_middle = gm_ref[...]
    grad_branch = grad_middle * vec[5:6, :]
    small = grad_branch.astype(BF)
    gb_ref[...] = small
    for r, w in enumerate((w0, w1, w2, w3)):
        gc_ref[r] = nt(small, w[...]).astype(BF)

    def add(k, values):
        sums[k : k + 1, :] += jnp.sum(values, axis=0, keepdims=True)

    add(0, grad_normed * scaled)
    add(1, grad_normed)
    add(2, grad_middle * bt[...])
    add(3, grad_branch)


def mid_call(sc, parts, cots, middle, branch, ws, vec):
    rows, width = middle.shape
    fw = width // 4
    tile = rows // 2

    def row(n):
        return pl.BlockSpec((tile, n), lambda i, sc: (i, 0))

    return pl.pallas_call(
        mid_kernel,
        grid_spec=pltpu.PrefetchScalarGridSpec(
            num_scalar_prefetch=1,
            grid=(2,),
            in_specs=[row(width)] * 3
            + [row(fw)] * 4
            + [row(width)] * 2
            + [whole_spec(ws[0].shape)] * 4
            + [whole_spec(vec.shape)],
            out_specs=[
                row(width),
                row(width),
                pl.BlockSpec((4, tile, fw), lambda i, sc: (0, i, 0)),
                whole_spec((8, width)),
            ],
        ),
        out_shape=[
            jax.ShapeDtypeStruct((rows, width), F32),
            jax.ShapeDtypeStruct((rows, width), BF),
            jax.ShapeDtypeStruct((4, rows, fw), BF),
            jax.ShapeDtypeStruct((8, width), F32),
        ],
        compiler_params=params(),
        name="mid",
        cost_estimate=costs(6),
    )(sc, *parts, *cots, middle, branch, *ws, vec)


def gn1_kernel(sc, gq0, gq1, gk, gv, w_ref, o0, o1, o2, o3):
    width = w_ref.shape[1] // 3
    query = jnp.concatenate([gq0[...], gq1[...]], axis=1)
    total = (
        nn(query, w_ref[:, 0:width])
        + nn(gk[...], w_ref[:, width : 2 * width])
        + nn(gv[...], w_ref[:, 2 * width : 3 * width])
    ).astype(BF)
    for r, ref in enumerate((o0, o1, o2, o3)):

        @pl.when(pl.program_id(0) == r)
        def _():
            ref[...] = total


def gn1_call(sc, gq0, gq1, gk, gv, w):
    rows = gk.shape[0]
    features, wide = w.shape
    sub = rows // 4

    def row(n):
        return pl.BlockSpec((sub, n), lambda r, sc: (sc[0] ^ r, 0))

    return pl.pallas_call(
        gn1_kernel,
        grid_spec=pltpu.PrefetchScalarGridSpec(
            num_scalar_prefetch=1,
            grid=(4,),
            in_specs=[row(PAIR), row(PAIR), row(features), row(features), whole_spec(w.shape)],
            out_specs=[whole_spec((sub, wide // 3))] * 4,
        ),
        out_shape=[jax.ShapeDtypeStruct((sub, wide // 3), BF)] * 4,
        compiler_params=params(),
        name="gn1",
        cost_estimate=costs(6),
    )(sc, gq0, gq1, gk, gv, w)


def qkvg_kernel(gq, gk, gv, n1, out):
    unit = out.shape[2]
    per = n1.shape[1] // unit
    for c, ref in enumerate((gq, gk, gv)):
        both = tn(ref[...], n1[...]).astype(BF)
        for k in range(per):
            out[c * per + k] = both[:, k * unit : (k + 1) * unit]


def qkvg_call(gq, gk, gv, n1):
    features = gq.shape[1]
    unit = n1.shape[1] // 8
    return pl.pallas_call(
        qkvg_kernel,
        out_shape=jax.ShapeDtypeStruct((24, features, unit), BF),
        compiler_params=params(0),
        name="qkv_grad",
        cost_estimate=costs(5),
    )(gq, gk, gv, n1)


def nsum_kernel(sc, a0, a1, a2, a3, x0, x1, x2, x3, sums):
    t = sc[0]
    r = pl.program_id(0)
    width = 4 * x0.shape[1]

    @pl.when(r == 0)
    def _():
        sums[...] = jnp.zeros(sums.shape, F32)

    value = jnp.concatenate(unxor([x[...].astype(F32) for x in (x0, x1, x2, x3)], t), axis=1)
    mean, rstd = stats_of([value], width)
    scaled = (value - mean) * rstd
    for k, ref in enumerate((a0, a1, a2, a3)):

        @pl.when(r == k)
        def _():
            part = ref[...].astype(F32)
            sums[0:1, :] += jnp.sum(part * scaled, axis=0, keepdims=True)
            sums[1:2, :] += jnp.sum(part, axis=0, keepdims=True)


def nsum_call(sc, pieces, xs):
    sub, width = pieces[0].shape
    fw = width // 4
    return pl.pallas_call(
        nsum_kernel,
        grid_spec=pltpu.PrefetchScalarGridSpec(
            num_scalar_prefetch=1,
            grid=(4,),
            in_specs=[whole_spec((sub, width))] * 4
            + [pl.BlockSpec((sub, fw), lambda r, sc: (sc[0] ^ r, 0))] * 4,
            out_specs=whole_spec((8, width)),
        ),
        out_shape=jax.ShapeDtypeStruct((8, width), F32),
        compiler_params=params(),
        name="norm_sums",
        cost_estimate=costs(5),
    )(sc, *pieces, *xs)


def last_kernel(sc, a0, a1, a2, x0, x1, x2, x3, gm, vec, o0, o1, o2, o3, scr):
    t = sc[0]
    fw = x0.shape[1]
    width = 4 * fw

    grad_normed = a0[...].astype(F32) + a1[...].astype(F32) + a2[...].astype(F32)
    chunks = unxor([x[...].astype(F32) for x in (x0, x1, x2, x3)], t)
    value = jnp.concatenate(chunks, axis=1)
    mean, rstd = stats_of([value], width)
    scaled = (value - mean) * rstd
    inner = grad_normed * vec[0:1, :]
    mean_a = jnp.sum(inner, axis=1, keepdims=True) / width
    mean_b = jnp.sum(inner * scaled, axis=1, keepdims=True) / width
    scr[...] = (gm[...] + rstd * (inner - mean_a - scaled * mean_b)).astype(BF)
    for r, ref in enumerate((o0, o1, o2, o3)):
        ref[...] = scr[:, pl.ds(pl.multiple_of((t ^ r) * fw, fw), fw)]


def last_call(sc, parts, xs, grad_middle, vec):
    rows, width = grad_middle.shape
    fw = width // 4
    tile = rows // 2

    def row(n):
        return pl.BlockSpec((tile, n), lambda i, sc: (i, 0))

    def mine(n):
        return pl.BlockSpec((tile, n), lambda i, sc: (sc[0] * 2 + i, 0))

    return pl.pallas_call(
        last_kernel,
        grid_spec=pltpu.PrefetchScalarGridSpec(
            num_scalar_prefetch=1,
            grid=(2,),
            in_specs=[row(width)] * 3 + [mine(fw)] * 4 + [row(width), whole_spec(vec.shape)],
            out_specs=[row(fw)] * 4,
            scratch_shapes=[pltpu.VMEM((tile, width), BF)],
        ),
        out_shape=[jax.ShapeDtypeStruct((rows, fw), BF)] * 4,
        compiler_params=params(),
        name="last",
        cost_estimate=costs(3),
    )(sc, *parts, *xs, grad_middle, vec)


def out_kernel(sc, a0, a1, a2, k0, k1, k2, k3, mid, vec, o0, o1, o2, o3, sums, scr):
    t = sc[0]
    fw = k0.shape[1]

    @pl.when(pl.program_id(0) == 0)
    def _():
        sums[...] = jnp.zeros(sums.shape, F32)

    total = a0[...].astype(F32) + a1[...].astype(F32) + a2[...].astype(F32) + vec[6:7, :]
    scr[...] = (mid[...] + vec[7:8, :] * total).astype(BF)
    for r, ref in enumerate((o0, o1, o2, o3)):
        ref[...] = scr[:, pl.ds(pl.multiple_of((t ^ r) * fw, fw), fw)]
    grad = jnp.concatenate(unxor([k[...].astype(F32) for k in (k0, k1, k2, k3)], t), axis=1)
    sums[0:1, :] += jnp.sum(grad * total, axis=0, keepdims=True)
    sums[1:2, :] += jnp.sum(grad * vec[7:8, :], axis=0, keepdims=True)


def out_call(sc, parts, cots, middle, vec):
    rows, width = middle.shape
    fw = width // 4
    tile = rows // 2

    def row(n):
        return pl.BlockSpec((tile, n), lambda i, sc: (i, 0))

    return pl.pallas_call(
        out_kernel,
        grid_spec=pltpu.PrefetchScalarGridSpec(
            num_scalar_prefetch=1,
            grid=(2,),
            in_specs=[row(width)] * 3 + [row(fw)] * 4 + [row(width), whole_spec(vec.shape)],
            out_specs=[row(fw)] * 4 + [whole_spec((8, width))],
            scratch_shapes=[pltpu.VMEM((tile, width), BF)],
        ),
        out_shape=[jax.ShapeDtypeStruct((rows, fw), BF)] * 4
        + [jax.ShapeDtypeStruct((8, width), F32)],
        compiler_params=params(),
        name="block_out",
        cost_estimate=costs(3),
    )(sc, *parts, *cots, middle, vec)


def after(*values):
    return lax.optimization_barrier(values)


def placed(pieces, t, axis):
    return jnp.concatenate(unxor(pieces, t), axis=axis)


def reduce4(pieces):
    far = (pieces[2].astype(F32) + px(pieces[3], 1).astype(F32)).astype(BF)
    return pieces[0], px(pieces[1], 1), px(far, 2)


def halved(blocks, s):
    for axis, bits, place in ((1, 2, 1), (1, 1, 0), (0, 4, 2)):
        mine = (s >> place) & 1
        keep = lax.dynamic_index_in_dim(blocks, mine, axis, keepdims=False)
        send = lax.dynamic_index_in_dim(blocks, 1 - mine, axis, keepdims=False)
        got = ps(send.astype(BF), bits)
        blocks = keep.astype(F32) + got.astype(F32)
    return blocks


def spans_of(image_ids, row_count, first_row, margin, near):
    tokens = image_ids.shape[0]
    most = tokens // IMG_LEAST + 1
    place = jnp.arange(tokens, dtype=jnp.int32)
    names = jnp.arange(most, dtype=jnp.int32)[:, None]
    same = image_ids[None, :] == names
    low = jnp.min(jnp.where(same, place[None, :], tokens), axis=1)
    high = jnp.max(jnp.where(same, place[None, :] + 1, 0), axis=1)
    own = lax.dynamic_slice_in_dim(image_ids, first_row, row_count, 0)
    mine = own[None, :] == names
    start = jnp.sum(jnp.where(mine, low[:, None], 0), axis=0)
    end = jnp.sum(jnp.where(mine, high[:, None], 0), axis=0)
    valid = own >= 0
    shift = margin - first_row
    start = jnp.where(valid, start + shift, 0)
    end = jnp.where(valid, end + shift, 0)
    lo = jnp.min(jnp.where(valid, start, near).reshape(-1, TILE), axis=1)
    hi = jnp.max(end.reshape(-1, TILE), axis=1)
    lo = jnp.clip(lo // TILE, 0, near // TILE)
    hi = jnp.clip(-(-hi // TILE), 0, near // TILE)
    spans = jnp.concatenate(
        [start[None, :], end[None, :], jnp.zeros((6, row_count), jnp.int32)], axis=0
    )
    return spans, jnp.stack([lo, hi], axis=1).reshape(-1)


def per_device(
    block_input,
    cotangent,
    image_ids,
    qkv_weight,
    proj_weight,
    fc1_weight,
    fc2_weight,
    norm1_gain,
    norm1_shift,
    q_bias,
    v_bias,
    proj_bias,
    scale_attn,
    norm2_gain,
    norm2_shift,
    fc1_bias,
    fc2_bias,
    scale_mlp,
):
    row_count, fw = block_input.shape
    n_seq = lax.axis_size("seq")
    width = 4 * fw
    features = qkv_weight.shape[0]
    sub = row_count // 4
    t = lax.axis_index("tensor").astype(jnp.int32)
    s = lax.axis_index("seq").astype(jnp.int32)
    reach = (IMG - 1 + row_count - 1) // row_count
    tile_rows = min(128, row_count)

    xs = gather4(block_input)
    if n_seq == 8:
        own = jnp.concatenate([qkv_weight, proj_weight], axis=1)
        z2, z4, z6 = ps(own, 2), ps(own, 4), ps(own, 6)
        found = [None] * 8
        for bits, piece in ((0, own), (2, z2), (4, z4), (6, z6)):
            found[bits] = piece
            found[bits ^ 1] = ps(piece, 1)
        w_qkv = jnp.zeros((8,) + own.shape, BF)
        for bits in range(8):
            w_qkv = lax.dynamic_update_slice(w_qkv, found[bits][None], (s ^ bits, 0, 0))
    else:
        w_qkv = jnp.concatenate(
            [
                lax.all_gather(w, "seq", axis=1, tiled=True)[None]
                for w in (qkv_weight, proj_weight)
            ],
            axis=2,
        )
    vec_own = jnp.stack(
        [
            norm1_gain,
            norm1_shift,
            norm2_gain,
            norm2_shift,
            proj_bias,
            scale_attn,
            fc2_bias,
            scale_mlp,
        ]
    )
    vec = placed([vec_own] + [px(vec_own, r) for r in range(1, 4)], t, 1)
    units = fc1_weight.shape[0]

    offsets_of = []
    counts = []
    for place in range(2 * reach + 1):
        offset = reach - place
        if offset == 0:
            count = row_count
        else:
            need = IMG - 1 - (abs(offset) - 1) * row_count
            count = min(row_count, -(-need // tile_rows) * tile_rows)
        offsets_of.append(offset)
        counts.append(count)
    offsets = [sum(counts[:k]) for k in range(len(counts))]
    near = sum(counts)
    margin = offsets[reach]
    spans, edges = spans_of(image_ids, row_count, s * row_count, margin, near)
    sc = jnp.concatenate([t[None], edges])
    sc_t = t[None]

    normed1, query, kv0, kv1, w_full, proj_full = qkv_call(
        sc_t, xs, w_qkv, vec, q_bias[None, :], v_bias[None, :]
    )
    nears = []
    for kv in (kv0, kv1):
        pieces = []
        for offset, count in zip(offsets_of, counts):
            if offset == 0:
                pieces.append(kv)
            elif offset > 0:
                pieces.append(passed_along(kv[row_count - count :], offset))
            else:
                pieces.append(passed_along(kv[:count], offset))
        nears.append(pieces)
    cots = swap4([rows_at(cotangent, t ^ r, sub) for r in range(4)])
    grad_second = (
        jnp.concatenate(unxor(cots, t), axis=1).astype(F32) * vec[7:8, :]
    ).astype(BF)
    grads = gather4(grad_second)
    contexts = []
    stats = []
    stacked = jnp.concatenate([fc1_weight, fc2_weight], axis=0)
    stacked, *nears[0] = after(stacked, *nears[0])
    others = lax.all_gather(stacked, "seq", axis=1, tiled=True)
    ws = gather4(proj_full)
    for pair in range(2):
        ctx, st = fwd_call(pair, sc, query, spans, nears[pair], offsets, counts)
        if pair == 0:
            ctx, *rest = after(ctx, *ws, *grads)
            ws, grads = rest[:4], rest[4:]
        contexts.append(ctx)
        stats.append(st)
    context = jnp.concatenate(contexts, axis=1)
    ctx_rows = swap4([rows_at(context, t ^ r, sub) for r in range(4)])
    branch, middle, normed2 = proj_call(sc_t, ctx_rows, ws, xs, vec)
    n_near = px(normed2, 1)
    n_across = px(normed2, 2)
    n_far = px(n_across, 1)
    bias1 = fc1_bias[None, :]
    hid_b, gb_b, s2, s3, d2, d3, fb_b = mlp_call((n_across, n_far), grads[2:], others, bias1)
    far = (d2.astype(F32) + px(d3, 1).astype(F32)).astype(BF)
    far, n_near = after(far, n_near)
    far = px(far, 2)
    hid_a, gb_a, s0, s1, d0, d1, fb_a = mlp_call((normed2, n_near), grads[:2], others, bias1)
    from_near = px(d1, 1)

    fc_part = wgrad_call((normed2, n_near, n_across, n_far), grads, (gb_a, gb_b), (hid_a, hid_b))
    far, fc_part = after(far, fc_part)
    fc_out = lax.psum_scatter(fc_part, "seq", scatter_dimension=0, tiled=True)
    grad_middle, grad_branch, grad_ctx, sums_mid = mid_call(
        sc_t, (d0, from_near, far), cots, middle, branch, ws, vec
    )
    grad_rows = jnp.stack(swap4([grad_ctx[r] for r in range(4)]))
    grad_rows, grad_branch, s0, s1, s2, s3 = after(grad_rows, grad_branch, s0, s1, s2, s3)
    seconds = reduce4([s0, s1, s2, s3])
    branch_all = gather4(grad_branch)

    grad_q = []
    grad_k = []
    grad_v = []
    for pair in range(2):
        got = bwd_call(
            pair, sc, query, spans, stats[pair], grad_rows, nears[pair], offsets, counts, reach
        )
        got = list(got)
        if pair == 0:
            got[1], grad_rows = after(got[1], grad_rows)
        if pair == 0:
            got[0], *branch_all = after(got[0], *branch_all)
            branch_rows = placed(branch_all, t, 0)
            proj_part = tn(branch_rows, context).astype(BF)
            if n_seq == 8:
                proj_out = halved(proj_part.reshape(2, 2, 2, width // 8, features), s)
            else:
                proj_out = lax.psum_scatter(proj_part, "seq", scatter_dimension=0, tiled=True)
        else:
            got[0], *seconds = after(got[0], *seconds)
            o0, o1, o2, o3, sums_out = out_call(sc_t, seconds, cots, middle, vec)
            block_output = placed(swap4([o0, o1, o2, o3]), t, 0)
        grad_q.append(got[0])
        backs = [
            passed_along(got[1 + k], -offset)
            for k, offset in enumerate(offsets_of)
            if offset != 0
        ]
        if pair == 1:
            *backs, block_output = after(*backs, block_output)
        total = got[1 + reach]
        others_of = [(o, c) for o, c in zip(offsets_of, counts) if o != 0]
        for back, (offset, count) in zip(backs, others_of):
            back = back.astype(F32)
            if count < row_count:
                gap = row_count - count
                ends = ((gap, 0), (0, 0)) if offset > 0 else ((0, gap), (0, 0))
                back = jnp.pad(back, ends)
            total = total + back
        total = total.astype(BF)
        grad_k.append(total[:, :PAIR])
        grad_v.append(total[:, PAIR:])
    gk = jnp.concatenate(grad_k, axis=1)
    gv = jnp.concatenate(grad_v, axis=1)
    gq = jnp.concatenate(grad_q, axis=1)
    if n_seq == 8:
        unit = width // 8
        blocks = qkvg_call(gq, gk, gv, normed1).reshape(2, 2, 2, 3, features, unit)
        blocks, gk = after(blocks, gk)
        blocks = halved(blocks, s)
        qkv_out = jnp.concatenate([blocks[k] for k in range(3)], axis=1)
    else:
        qkv_parts = [tn(g, normed1) for g in (gq, gk, gv)]
        qkv_out = lax.psum_scatter(
            jnp.stack(qkv_parts, axis=1).reshape(features, 3 * width).astype(BF),
            "seq",
            scatter_dimension=1,
            tiled=True,
        ).astype(F32)
    pieces = gn1_call(sc_t, grad_q[0], grad_q[1], gk, gv, w_full)
    sums_last = nsum_call(sc_t, pieces, xs)
    i0, i1, i2, i3 = last_call(sc_t, reduce4(pieces), xs, grad_middle, vec)
    rows8 = jnp.concatenate([sums_last[0:2], sums_mid[0:4], sums_out[0:2]], axis=0)
    cut = [lax.dynamic_slice_in_dim(rows8, (t ^ r) * fw, fw, 1) for r in range(4)]
    got = swap4(cut)
    own8 = got[0] + got[1] + got[2] + got[3]
    flat = jnp.concatenate(
        [
            own8.reshape(-1),
            jnp.sum(gq.astype(F32), axis=0),
            jnp.sum(gv.astype(F32), axis=0),
            fb_a[0] + fb_b[0],
        ]
    ).reshape(-1, 128)
    flat, i0, i1, i2, i3 = after(flat, i0, i1, i2, i3)
    input_grad = placed(swap4([i0, i1, i2, i3]), t, 0)
    if n_seq == 8:
        for bits in (2, 1, 4):
            flat = flat + ps(flat, bits)
    else:
        flat = lax.psum(flat, "seq")
    flat = flat.reshape(-1)
    own8 = flat[: 8 * fw].reshape(8, fw)
    q_bias_grad = flat[8 * fw : 8 * fw + features]
    v_bias_grad = flat[8 * fw + features : 8 * fw + 2 * features]
    fc1_bias_grad = flat[8 * fw + 2 * features :]
    return (
        block_output,
        input_grad,
        qkv_out,
        proj_out.T.astype(F32),
        fc_out[:, :units].T.astype(F32),
        fc_out[:, units:].T.astype(F32),
        own8[0],
        own8[1],
        q_bias_grad,
        v_bias_grad,
        own8[5],
        own8[4],
        own8[2],
        own8[3],
        fc1_bias_grad,
        own8[7],
        own8[6],
    )


def solution(mesh):
    cut = P("tensor", "seq")
    by_tensor = P("tensor")
    in_specs = (P("seq", "tensor"), P("seq", "tensor"), P()) + (cut,) * 4 + (by_tensor,) * 11
    out_specs = (P("seq", "tensor"), P("seq", "tensor")) + (cut,) * 4 + (by_tensor,) * 11

    return jax.shard_map(
        per_device, mesh=mesh, in_specs=in_specs, out_specs=out_specs, check_vma=False
    )
```

```python
import functools

import jax
import jax.numpy as jnp
from jax import lax
from jax.experimental import pallas as pl
from jax.experimental.pallas import tpu as pltpu
from jax.sharding import PartitionSpec as P


HEAD_DIM = 64
IMG = 1370
IMG_LEAST = 686
EPS = 1e-06
NEG = -1e30
BF = jnp.bfloat16
F32 = jnp.float32
TILE = 256
STEP = 2 * TILE
PAIR = 2 * HEAD_DIM
SCALE = HEAD_DIM ** (-0.5)
INV_SQRT2 = 0.7071067811865476
INV_SQRT2PI = 0.3989422804014327


def px(value, bits):
    pairs = [(i, i ^ bits) for i in range(lax.axis_size("tensor"))]
    return lax.ppermute(value, "tensor", pairs)


def ps(value, bits):
    pairs = [(i, i ^ bits) for i in range(lax.axis_size("seq"))]
    return lax.ppermute(value, "seq", pairs)


def passed_along(block, distance):
    devices = range(lax.axis_size("seq"))
    route = [(i - distance, i) for i in devices if i - distance in devices]
    return lax.ppermute(block, "seq", route)


def gather4(value):
    across = px(value, 2)
    return [value, px(value, 1), across, px(across, 1)]


def swap4(pieces):
    return [pieces[0]] + [px(pieces[r], r) for r in range(1, 4)]


def rows_at(value, index, size):
    return lax.dynamic_slice_in_dim(value, index * size, size, 0)


def unxor(pieces, t):
    low = (t & 1) == 1
    high = (t & 2) == 2
    first = [jnp.where(low, pieces[r ^ 1], pieces[r]) for r in range(4)]
    return [jnp.where(high, first[r ^ 2], first[r]) for r in range(4)]


def nt(left, right):
    return lax.dot_general(left, right, (((1,), (1,)), ((), ())), preferred_element_type=F32)


def nn(left, right):
    return lax.dot_general(left, right, (((1,), (0,)), ((), ())), preferred_element_type=F32)


def tn(left, right):
    return lax.dot_general(left, right, (((0,), (0,)), ((), ())), preferred_element_type=F32)


def params(n=1, limit=56):
    return pltpu.CompilerParams(
        dimension_semantics=("arbitrary",) * n, vmem_limit_bytes=limit * 1024 * 1024
    )


def costs(micros):
    return pl.CostEstimate(flops=int(micros * 1e9), transcendentals=0, bytes_accessed=1 << 20)


def stats_of(chunks, width):
    total = sum(jnp.sum(c, axis=1, keepdims=True) for c in chunks)
    square = sum(jnp.sum(c * c, axis=1, keepdims=True) for c in chunks)
    mean = total / width
    rstd = lax.rsqrt(square / width - mean * mean + EPS)
    return mean, rstd


def qkv_kernel(sc, x0, x1, x2, x3, w_ref, vec, qb, vb, n1_ref, q_ref, kv0_ref, kv1_ref, wout, wproj, wscr):
    groups = w_ref.shape[0]
    part = w_ref.shape[2] * 3 // 4
    small = w_ref.shape[2] - part

    @pl.when(pl.program_id(0) == 0)
    def _():
        for g in range(groups):
            wscr[:, g * part : (g + 1) * part] = w_ref[g, :, :part]
            wproj[:, g * small : (g + 1) * small] = w_ref[g, :, part:]
        wout[...] = wscr[...]

    t = sc[0]
    chunks = unxor([r[...].astype(F32) for r in (x0, x1, x2, x3)], t)
    fw = x0.shape[1]
    width = 4 * fw
    mean, rstd = stats_of(chunks, width)
    for a in range(4):
        lo = a * fw
        scaled = (chunks[a] - mean) * rstd
        n1_ref[:, lo : lo + fw] = (
            scaled * vec[0:1, lo : lo + fw] + vec[1:2, lo : lo + fw]
        ).astype(BF)
    normed = n1_ref[...]
    query = nt(normed, wscr[:, 0:width]) + qb[...]
    q_ref[...] = query.astype(BF)
    key = nt(normed, wscr[:, width : 2 * width]).astype(BF)
    value = (nt(normed, wscr[:, 2 * width : 3 * width]) + vb[...]).astype(BF)
    for p, ref in enumerate((kv0_ref, kv1_ref)):
        ref[:, 0:PAIR] = key[:, p * PAIR : (p + 1) * PAIR]
        ref[:, PAIR : 2 * PAIR] = value[:, p * PAIR : (p + 1) * PAIR]


def qkv_call(sc, xs, w, vec, qb, vb):
    rows, fw = xs[0].shape
    groups, features, part = w.shape
    part = part * 3 // 4
    width = 4 * fw
    tile = TILE

    def full(shape):
        return pl.BlockSpec(shape, lambda i, sc: (0,) * len(shape))

    def row(n):
        return pl.BlockSpec((tile, n), lambda i, sc: (i, 0))

    return pl.pallas_call(
        qkv_kernel,
        grid_spec=pltpu.PrefetchScalarGridSpec(
            num_scalar_prefetch=1,
            grid=(rows // tile,),
            in_specs=[row(fw)] * 4
            + [full(w.shape), full(vec.shape), full(qb.shape), full(vb.shape)],
            out_specs=[
                row(width),
                row(features),
                row(2 * PAIR),
                row(2 * PAIR),
                full((features, groups * part)),
                full((features, width)),
            ],
            scratch_shapes=[pltpu.VMEM((features, groups * part), BF)],
        ),
        out_shape=[
            jax.ShapeDtypeStruct((rows, width), BF),
            jax.ShapeDtypeStruct((rows, features), BF),
            jax.ShapeDtypeStruct((rows, 2 * PAIR), BF),
            jax.ShapeDtypeStruct((rows, 2 * PAIR), BF),
            jax.ShapeDtypeStruct((features, groups * part), BF),
            jax.ShapeDtypeStruct((features, width), BF),
        ],
        compiler_params=params(),
        name="qkv",
        cost_estimate=costs(7),
    )(sc, *xs, w, vec, qb, vb)


def load_pieces(pieces, target, sem, offsets, counts):
    copies = [
        pltpu.make_async_copy(ref, target.at[pl.ds(offset, count), :], sem.at[k])
        for k, (ref, offset, count) in enumerate(zip(pieces, offsets, counts))
    ]
    for copy in copies:
        copy.start()
    last = offsets[-1] + counts[-1]
    target[last:, :] = jnp.zeros((target.shape[0] - last, target.shape[1]), target.dtype)
    for copy in copies:
        copy.wait()


def by_head(values):
    lane = lax.broadcasted_iota(jnp.int32, values.shape, 1)
    first = jnp.where(lane < HEAD_DIM, values, 0.0)
    second = jnp.where(lane < HEAD_DIM, 0.0, values)
    return jnp.concatenate([first, second], axis=0).astype(BF)


def joined(values):
    return jnp.concatenate([values[0:HEAD_DIM, :TILE], values[HEAD_DIM:PAIR, TILE:]], axis=0)


def step_rows(lo, j):
    return pl.ds(pl.multiple_of(lo * TILE + j * STEP, TILE), STEP)


def scores_of(kv, head_query, lo, j, start, end):
    raw = nt(kv[step_rows(lo, j), 0:PAIR], head_query)
    place = lax.broadcasted_iota(jnp.int32, raw.shape, 0) + (lo * TILE + j * STEP)
    return jnp.where((place >= start) & (place < end), raw, NEG)


def fold8(values, how):
    return how(values.reshape(values.shape[0] // 8, 8, values.shape[1]), axis=0)


def twice(row):
    return jnp.concatenate([row, row], axis=1)


def fwd_kernel(offsets, counts, sc, q_ref, se_ref, *refs):
    n = len(counts)
    pieces = refs[:n]
    ctx_ref, st_ref, kv, s_scr, acc, sem = refs[n:]
    i = pl.program_id(0)

    @pl.when(i == 0)
    def _():
        load_pieces(pieces, kv, sem, offsets, counts)

    lo = sc[1 + 2 * i]
    steps = (sc[2 + 2 * i] - lo + 1) // 2
    start = twice(se_ref[0:1, :])
    end = twice(se_ref[1:2, :])
    head_query = by_head(q_ref[...].astype(F32) * SCALE)

    def first(j, peak):
        score = scores_of(kv, head_query, lo, j, start, end)
        s_scr[j] = score
        return jnp.maximum(peak, fold8(score, jnp.max))

    peak8 = lax.fori_loop(0, steps, first, jnp.full((8, 2 * TILE), NEG, F32))
    peak = jnp.max(peak8, axis=0, keepdims=True)
    peak = jnp.maximum(peak, 0.1 * NEG)

    def second(j, total):
        expon = jnp.exp(s_scr[j] - peak)
        s_scr[j] = expon
        return total + fold8(expon, jnp.sum)

    total8 = lax.fori_loop(0, steps, second, jnp.zeros((8, 2 * TILE), F32))
    total = jnp.sum(total8, axis=0, keepdims=True)
    inverse = 1.0 / jnp.where(end > start, total, 1.0)
    acc[...] = jnp.zeros(acc.shape, F32)

    def third(j, carry):
        prob = (s_scr[j] * inverse).astype(BF)
        vals = kv[step_rows(lo, j), PAIR : 2 * PAIR]
        acc[...] += tn(vals, prob)
        return carry

    lax.fori_loop(0, steps, third, 0)
    for head in range(2):
        at = slice(head * TILE, (head + 1) * TILE)
        st_ref[head : head + 1, :] = peak[:, at]
        st_ref[2 + head : 3 + head, :] = inverse[:, at]
    ctx_ref[...] = joined(acc[...]).T.astype(BF)


def fwd_call(pair, sc, query, spans, pieces, offsets, counts):
    rows = query.shape[0]
    near = sum(counts)
    return pl.pallas_call(
        functools.partial(fwd_kernel, offsets, counts),
        grid_spec=pltpu.PrefetchScalarGridSpec(
            num_scalar_prefetch=1,
            grid=(rows // TILE,),
            in_specs=[
                pl.BlockSpec((TILE, PAIR), lambda i, sc: (i, pair)),
                pl.BlockSpec((8, TILE), lambda i, sc: (0, i)),
            ]
            + [pl.BlockSpec(memory_space=pl.ANY)] * len(pieces),
            out_specs=[
                pl.BlockSpec((TILE, PAIR), lambda i, sc: (i, 0)),
                pl.BlockSpec((8, TILE), lambda i, sc: (0, i)),
            ],
            scratch_shapes=[
                pltpu.VMEM((near + TILE, 2 * PAIR), BF),
                pltpu.VMEM((near // STEP + 1, STEP, 2 * TILE), F32),
                pltpu.VMEM((PAIR, 2 * TILE), F32),
                pltpu.SemaphoreType.DMA((len(pieces),)),
            ],
        ),
        out_shape=[
            jax.ShapeDtypeStruct((rows, PAIR), BF),
            jax.ShapeDtypeStruct((8, rows), F32),
        ],
        compiler_params=params(),
        name="attn_fwd",
        cost_estimate=costs(17),
    )(sc, query, spans, *pieces)


def bwd_kernel(offsets, counts, sc, q_ref, se_ref, st_ref, g_ref, *refs):
    n = len(counts)
    pieces = refs[:n]
    dq_ref = refs[n]
    outs = refs[n + 1 : 2 * n + 1]
    kv, w_scr, g_scr, acc, dq_scr, sem = refs[2 * n + 1 :]
    r = pl.program_id(0)

    @pl.when(r == 0)
    def _():
        load_pieces(pieces, kv, sem, offsets, counts)
        acc[...] = jnp.zeros(acc.shape, F32)

    i = sc[0] ^ r
    lo = sc[1 + 2 * i]
    steps = (sc[2 + 2 * i] - lo + 1) // 2
    start = se_ref[0:1, :]
    end = se_ref[1:2, :]
    start = twice(start)
    end = twice(end)
    head_query = by_head(q_ref[...].astype(F32) * SCALE)
    head_grad = by_head(g_ref[0].astype(F32))
    peak = jnp.concatenate([st_ref[0:1, :], st_ref[1:2, :]], axis=1)
    inverse = jnp.concatenate([st_ref[2:3, :], st_ref[3:4, :]], axis=1)

    def first(j, dot8):
        score = scores_of(kv, head_query, lo, j, start, end)
        weight = jnp.exp(score - peak) * inverse
        vals = kv[step_rows(lo, j), PAIR : 2 * PAIR]
        grad_prob = nt(vals, head_grad)
        w_scr[j] = weight
        g_scr[j] = grad_prob
        return dot8 + fold8(weight * grad_prob, jnp.sum)

    dot8 = lax.fori_loop(0, steps, first, jnp.zeros((8, 2 * TILE), F32))
    rowdot = jnp.sum(dot8, axis=0, keepdims=True)
    dq_scr[...] = jnp.zeros(dq_scr.shape, F32)

    def second(j, carry):
        weight = w_scr[j]
        grad_score = (weight * (g_scr[j] - rowdot)).astype(BF)
        prob = weight.astype(BF)
        at = step_rows(lo, j)
        acc[at, 0:PAIR] += nn(grad_score, head_query)
        acc[at, PAIR : 2 * PAIR] += nn(prob, head_grad)
        dq_scr[...] += tn(kv[at, 0:PAIR], grad_score)
        return carry

    lax.fori_loop(0, steps, second, 0)
    dq_ref[...] = (joined(dq_scr[...]).T * SCALE).astype(BF)

    @pl.when(r == pl.num_programs(0) - 1)
    def _():
        for k in range(n):
            piece = acc[offsets[k] : offsets[k] + counts[k], :]
            outs[k][...] = piece.astype(outs[k].dtype)


def bwd_call(pair, sc, query, spans, stats, grads, pieces, offsets, counts, own):
    rows = query.shape[0]
    near = sum(counts)

    def whole(count):
        return pl.BlockSpec((count, 2 * PAIR), lambda r, sc: (0, 0))

    return pl.pallas_call(
        functools.partial(bwd_kernel, offsets, counts),
        grid_spec=pltpu.PrefetchScalarGridSpec(
            num_scalar_prefetch=1,
            grid=(rows // TILE,),
            in_specs=[
                pl.BlockSpec((TILE, PAIR), lambda r, sc: (sc[0] ^ r, pair)),
                pl.BlockSpec((8, TILE), lambda r, sc: (0, sc[0] ^ r)),
                pl.BlockSpec((8, TILE), lambda r, sc: (0, sc[0] ^ r)),
                pl.BlockSpec((1, TILE, PAIR), lambda r, sc: (r, 0, pair)),
            ]
            + [pl.BlockSpec(memory_space=pl.ANY)] * len(pieces),
            out_specs=[pl.BlockSpec((TILE, PAIR), lambda r, sc: (sc[0] ^ r, 0))]
            + [whole(c) for c in counts],
            scratch_shapes=[
                pltpu.VMEM((near + TILE, 2 * PAIR), BF),
                pltpu.VMEM((near // STEP + 1, STEP, 2 * TILE), F32),
                pltpu.VMEM((near // STEP + 1, STEP, 2 * TILE), F32),
                pltpu.VMEM((near + TILE, 2 * PAIR), F32),
                pltpu.VMEM((PAIR, 2 * TILE), F32),
                pltpu.SemaphoreType.DMA((len(pieces),)),
            ],
        ),
        out_shape=[jax.ShapeDtypeStruct((rows, PAIR), BF)]
        + [
            jax.ShapeDtypeStruct((c, 2 * PAIR), F32 if k == own else BF)
            for k, c in enumerate(counts)
        ],
        compiler_params=params(),
        name="attn_bwd",
        cost_estimate=costs(22),
    )(sc, query, spans, stats, grads, *pieces)


def whole_spec(shape):
    return pl.BlockSpec(shape, lambda i, sc: (0,) * len(shape))


def proj_kernel(sc, c0, c1, c2, c3, w0, w1, w2, w3, x0, x1, x2, x3, vec, bt_ref, mid_ref, n2_ref):
    t = sc[0]
    fw = x0.shape[1]
    branch = vec[4:5, :] + sum(
        nn(c[...], w[...]) for c, w in ((c0, w0), (c1, w1), (c2, w2), (c3, w3))
    )
    bt_ref[...] = branch
    chunks = unxor([x[...].astype(F32) for x in (x0, x1, x2, x3)], t)
    for a in range(4):
        at = slice(a * fw, (a + 1) * fw)
        mid_ref[:, at] = chunks[a] + vec[5:6, at] * branch[:, at]
    middle = mid_ref[...]
    mean, rstd = stats_of([middle], 4 * fw)
    n2_ref[...] = ((middle - mean) * rstd * vec[2:3, :] + vec[3:4, :]).astype(BF)


def proj_call(sc, contexts, ws, xs, vec):
    rows, fw = contexts[0].shape
    width = ws[0].shape[1]
    tile = rows // 2

    def row(n):
        return pl.BlockSpec((tile, n), lambda i, sc: (i, 0))

    def mine(n):
        return pl.BlockSpec((tile, n), lambda i, sc: (sc[0] * 2 + i, 0))

    return pl.pallas_call(
        proj_kernel,
        grid_spec=pltpu.PrefetchScalarGridSpec(
            num_scalar_prefetch=1,
            grid=(2,),
            in_specs=[row(fw)] * 4
            + [whole_spec(ws[0].shape)] * 4
            + [mine(fw)] * 4
            + [whole_spec(vec.shape)],
            out_specs=[row(width)] * 3,
        ),
        out_shape=[
            jax.ShapeDtypeStruct((rows, width), F32),
            jax.ShapeDtypeStruct((rows, width), F32),
            jax.ShapeDtypeStruct((rows, width), BF),
        ],
        compiler_params=params(),
        name="proj",
        cost_estimate=costs(4),
    )(sc, *contexts, *ws, *xs, vec)


def mlp_kernel(n0, n1, g0, g1, fc1, fc2, bias, h_ref, gb_ref, s0, s1, d0, d1, fb_ref):
    i = pl.program_id(0)
    step = 256
    hidden_units = fc1.shape[0]

    @pl.when(i == 0)
    def _():
        fb_ref[...] = jnp.zeros(fb_ref.shape, F32)

    def work(n_ref, g_ref, s_ref, d_ref):
        normed = n_ref[...]
        grads = g_ref[...]
        for u in range(hidden_units // step):
            at = slice(u * step, (u + 1) * step)
            before = nt(normed, fc1[at, :]) + bias[:, at]
            phi = 0.5 * (1.0 + lax.erf(before * INV_SQRT2))
            h_ref[:, at] = (before * phi).astype(BF)
            slope = phi + before * (jnp.exp(-0.5 * before * before) * INV_SQRT2PI)
            grad_before = (slope * nt(grads, fc2[at, :])).astype(BF)
            gb_ref[:, at] = grad_before
            wide = grad_before.astype(F32)
            fb_ref[0:1, at] += jnp.sum(wide, axis=0, keepdims=True)
        d_ref[...] = nn(gb_ref[...], fc1[...]).astype(BF)
        s_ref[...] = nn(h_ref[...], fc2[...]).astype(BF)

    @pl.when(i == 0)
    def _():
        work(n0, g0, s0, d0)

    @pl.when(i == 1)
    def _():
        work(n1, g1, s1, d1)


def mlp_call(normed, grads, weights, bias):
    rows, width = normed[0].shape
    hidden_units = bias.shape[1]

    def full(shape):
        return pl.BlockSpec(shape, lambda i: (0,) * len(shape))

    piece = jax.ShapeDtypeStruct((rows, width), BF)
    return pl.pallas_call(
        mlp_kernel,
        grid=(2,),
        in_specs=[full((rows, width))] * 4
        + [
            pl.BlockSpec((hidden_units, width), lambda i: (0, 0)),
            pl.BlockSpec((hidden_units, width), lambda i: (1, 0)),
            full(bias.shape),
        ],
        out_specs=[pl.BlockSpec((rows, hidden_units), lambda i: (i, 0))] * 2
        + [full((rows, width))] * 4
        + [full((8, hidden_units))],
        out_shape=[jax.ShapeDtypeStruct((2 * rows, hidden_units), BF)] * 2
        + [piece] * 4
        + [jax.ShapeDtypeStruct((8, hidden_units), F32)],
        compiler_params=params(),
        name="mlp",
        cost_estimate=costs(10),
    )(*normed, *grads, weights, weights, bias)


def wgrad_kernel(n0, n1, n2, n3, g0, g1, g2, g3, ba, bb, ha, hb, out):
    hidden_units = ba.shape[1]
    for k, (lefts, rights) in enumerate((((n0, n1, n2, n3), (ba, bb)), ((g0, g1, g2, g3), (ha, hb)))):
        total = 0.0
        for half in range(2):
            left = jnp.concatenate([lefts[2 * half][...], lefts[2 * half + 1][...]], axis=0)
            total = total + tn(left, rights[half][...])
        out[:, k * hidden_units : (k + 1) * hidden_units] = total.astype(BF)


def wgrad_call(normed, grads, befores, hiddens):
    sub, width = normed[0].shape
    rows, hidden_units = befores[0].shape
    tile = TILE

    def left():
        return pl.BlockSpec((sub, tile), lambda i: (0, i))

    def right():
        return pl.BlockSpec((rows, hidden_units), lambda i: (0, 0))

    return pl.pallas_call(
        wgrad_kernel,
        grid=(width // tile,),
        in_specs=[left()] * 8 + [right()] * 4,
        out_specs=pl.BlockSpec((tile, 2 * hidden_units), lambda i: (i, 0)),
        out_shape=jax.ShapeDtypeStruct((width, 2 * hidden_units), BF),
        compiler_params=params(),
        name="wgrads",
        cost_estimate=costs(9),
    )(*normed, *grads, *befores, *hiddens)


def mid_kernel(
    sc, a0, a1, a2, k0, k1, k2, k3, mid, bt, w0, w1, w2, w3, vec, gm_ref, gb_ref, gc_ref, sums
):
    t = sc[0]
    fw = k0.shape[1]
    width = 4 * fw

    @pl.when(pl.program_id(0) == 0)
    def _():
        sums[...] = jnp.zeros(sums.shape, F32)

    grad_normed = a0[...].astype(F32) + a1[...].astype(F32) + a2[...].astype(F32)
    middle = mid[...]
    mean, rstd = stats_of([middle], width)
    scaled = (middle - mean) * rstd
    inner = grad_normed * vec[2:3, :]
    mean_a = jnp.sum(inner, axis=1, keepdims=True) / width
    mean_b = jnp.sum(inner * scaled, axis=1, keepdims=True) / width
    chunks = unxor([k[...].astype(F32) for k in (k0, k1, k2, k3)], t)
    back = rstd * (inner - mean_a - scaled * mean_b)
    for a in range(4):
        at = slice(a * fw, (a + 1) * fw)
        gm_ref[:, at] = chunks[a] + back[:, at]
    grad_middle = gm_ref[...]
    grad_branch = grad_middle * vec[5:6, :]
    small = grad_branch.astype(BF)
    gb_ref[...] = small
    for r, w in enumerate((w0, w1, w2, w3)):
        gc_ref[r] = nt(small, w[...]).astype(BF)

    def add(k, values):
        sums[k : k + 1, :] += jnp.sum(values, axis=0, keepdims=True)

    add(0, grad_normed * scaled)
    add(1, grad_normed)
    add(2, grad_middle * bt[...])
    add(3, grad_branch)


def mid_call(sc, parts, cots, middle, branch, ws, vec):
    rows, width = middle.shape
    fw = width // 4
    tile = rows // 2

    def row(n):
        return pl.BlockSpec((tile, n), lambda i, sc: (i, 0))

    return pl.pallas_call(
        mid_kernel,
        grid_spec=pltpu.PrefetchScalarGridSpec(
            num_scalar_prefetch=1,
            grid=(2,),
            in_specs=[row(width)] * 3
            + [row(fw)] * 4
            + [row(width)] * 2
            + [whole_spec(ws[0].shape)] * 4
            + [whole_spec(vec.shape)],
            out_specs=[
                row(width),
                row(width),
                pl.BlockSpec((4, tile, fw), lambda i, sc: (0, i, 0)),
                whole_spec((8, width)),
            ],
        ),
        out_shape=[
            jax.ShapeDtypeStruct((rows, width), F32),
            jax.ShapeDtypeStruct((rows, width), BF),
            jax.ShapeDtypeStruct((4, rows, fw), BF),
            jax.ShapeDtypeStruct((8, width), F32),
        ],
        compiler_params=params(),
        name="mid",
        cost_estimate=costs(6),
    )(sc, *parts, *cots, middle, branch, *ws, vec)


def gn1_kernel(sc, gq0, gq1, gk, gv, w_ref, o0, o1, o2, o3):
    width = w_ref.shape[1] // 3
    query = jnp.concatenate([gq0[...], gq1[...]], axis=1)
    total = (
        nn(query, w_ref[:, 0:width])
        + nn(gk[...], w_ref[:, width : 2 * width])
        + nn(gv[...], w_ref[:, 2 * width : 3 * width])
    ).astype(BF)
    for r, ref in enumerate((o0, o1, o2, o3)):

        @pl.when(pl.program_id(0) == r)
        def _():
            ref[...] = total


def gn1_call(sc, gq0, gq1, gk, gv, w):
    rows = gk.shape[0]
    features, wide = w.shape
    sub = rows // 4

    def row(n):
        return pl.BlockSpec((sub, n), lambda r, sc: (sc[0] ^ r, 0))

    return pl.pallas_call(
        gn1_kernel,
        grid_spec=pltpu.PrefetchScalarGridSpec(
            num_scalar_prefetch=1,
            grid=(4,),
            in_specs=[row(PAIR), row(PAIR), row(features), row(features), whole_spec(w.shape)],
            out_specs=[whole_spec((sub, wide // 3))] * 4,
        ),
        out_shape=[jax.ShapeDtypeStruct((sub, wide // 3), BF)] * 4,
        compiler_params=params(),
        name="gn1",
        cost_estimate=costs(6),
    )(sc, gq0, gq1, gk, gv, w)


def qkvg_kernel(gq, gk, gv, n1, out):
    unit = out.shape[2]
    per = n1.shape[1] // unit
    for c, ref in enumerate((gq, gk, gv)):
        both = tn(ref[...], n1[...]).astype(BF)
        for k in range(per):
            out[c * per + k] = both[:, k * unit : (k + 1) * unit]


def qkvg_call(gq, gk, gv, n1):
    features = gq.shape[1]
    unit = n1.shape[1] // 8
    return pl.pallas_call(
        qkvg_kernel,
        out_shape=jax.ShapeDtypeStruct((24, features, unit), BF),
        compiler_params=params(0),
        name="qkv_grad",
        cost_estimate=costs(5),
    )(gq, gk, gv, n1)


def nsum_kernel(sc, a0, a1, a2, a3, x0, x1, x2, x3, sums):
    t = sc[0]
    r = pl.program_id(0)
    width = 4 * x0.shape[1]

    @pl.when(r == 0)
    def _():
        sums[...] = jnp.zeros(sums.shape, F32)

    value = jnp.concatenate(unxor([x[...].astype(F32) for x in (x0, x1, x2, x3)], t), axis=1)
    mean, rstd = stats_of([value], width)
    scaled = (value - mean) * rstd
    for k, ref in enumerate((a0, a1, a2, a3)):

        @pl.when(r == k)
        def _():
            part = ref[...].astype(F32)
            sums[0:1, :] += jnp.sum(part * scaled, axis=0, keepdims=True)
            sums[1:2, :] += jnp.sum(part, axis=0, keepdims=True)


def nsum_call(sc, pieces, xs):
    sub, width = pieces[0].shape
    fw = width // 4
    return pl.pallas_call(
        nsum_kernel,
        grid_spec=pltpu.PrefetchScalarGridSpec(
            num_scalar_prefetch=1,
            grid=(4,),
            in_specs=[whole_spec((sub, width))] * 4
            + [pl.BlockSpec((sub, fw), lambda r, sc: (sc[0] ^ r, 0))] * 4,
            out_specs=whole_spec((8, width)),
        ),
        out_shape=jax.ShapeDtypeStruct((8, width), F32),
        compiler_params=params(),
        name="norm_sums",
        cost_estimate=costs(5),
    )(sc, *pieces, *xs)


def last_kernel(sc, a0, a1, a2, x0, x1, x2, x3, gm, vec, o0, o1, o2, o3, scr):
    t = sc[0]
    fw = x0.shape[1]
    width = 4 * fw

    grad_normed = a0[...].astype(F32) + a1[...].astype(F32) + a2[...].astype(F32)
    chunks = unxor([x[...].astype(F32) for x in (x0, x1, x2, x3)], t)
    value = jnp.concatenate(chunks, axis=1)
    mean, rstd = stats_of([value], width)
    scaled = (value - mean) * rstd
    inner = grad_normed * vec[0:1, :]
    mean_a = jnp.sum(inner, axis=1, keepdims=True) / width
    mean_b = jnp.sum(inner * scaled, axis=1, keepdims=True) / width
    scr[...] = (gm[...] + rstd * (inner - mean_a - scaled * mean_b)).astype(BF)
    for r, ref in enumerate((o0, o1, o2, o3)):
        ref[...] = scr[:, pl.ds(pl.multiple_of((t ^ r) * fw, fw), fw)]


def last_call(sc, parts, xs, grad_middle, vec):
    rows, width = grad_middle.shape
    fw = width // 4
    tile = rows // 2

    def row(n):
        return pl.BlockSpec((tile, n), lambda i, sc: (i, 0))

    def mine(n):
        return pl.BlockSpec((tile, n), lambda i, sc: (sc[0] * 2 + i, 0))

    return pl.pallas_call(
        last_kernel,
        grid_spec=pltpu.PrefetchScalarGridSpec(
            num_scalar_prefetch=1,
            grid=(2,),
            in_specs=[row(width)] * 3 + [mine(fw)] * 4 + [row(width), whole_spec(vec.shape)],
            out_specs=[row(fw)] * 4,
            scratch_shapes=[pltpu.VMEM((tile, width), BF)],
        ),
        out_shape=[jax.ShapeDtypeStruct((rows, fw), BF)] * 4,
        compiler_params=params(),
        name="last",
        cost_estimate=costs(3),
    )(sc, *parts, *xs, grad_middle, vec)


def out_kernel(sc, a0, a1, a2, k0, k1, k2, k3, mid, vec, o0, o1, o2, o3, sums, scr):
    t = sc[0]
    fw = k0.shape[1]

    @pl.when(pl.program_id(0) == 0)
    def _():
        sums[...] = jnp.zeros(sums.shape, F32)

    total = a0[...].astype(F32) + a1[...].astype(F32) + a2[...].astype(F32) + vec[6:7, :]
    scr[...] = (mid[...] + vec[7:8, :] * total).astype(BF)
    for r, ref in enumerate((o0, o1, o2, o3)):
        ref[...] = scr[:, pl.ds(pl.multiple_of((t ^ r) * fw, fw), fw)]
    grad = jnp.concatenate(unxor([k[...].astype(F32) for k in (k0, k1, k2, k3)], t), axis=1)
    sums[0:1, :] += jnp.sum(grad * total, axis=0, keepdims=True)
    sums[1:2, :] += jnp.sum(grad * vec[7:8, :], axis=0, keepdims=True)


def out_call(sc, parts, cots, middle, vec):
    rows, width = middle.shape
    fw = width // 4
    tile = rows // 2

    def row(n):
        return pl.BlockSpec((tile, n), lambda i, sc: (i, 0))

    return pl.pallas_call(
        out_kernel,
        grid_spec=pltpu.PrefetchScalarGridSpec(
            num_scalar_prefetch=1,
            grid=(2,),
            in_specs=[row(width)] * 3 + [row(fw)] * 4 + [row(width), whole_spec(vec.shape)],
            out_specs=[row(fw)] * 4 + [whole_spec((8, width))],
            scratch_shapes=[pltpu.VMEM((tile, width), BF)],
        ),
        out_shape=[jax.ShapeDtypeStruct((rows, fw), BF)] * 4
        + [jax.ShapeDtypeStruct((8, width), F32)],
        compiler_params=params(),
        name="block_out",
        cost_estimate=costs(3),
    )(sc, *parts, *cots, middle, vec)


def after(*values):
    return lax.optimization_barrier(values)


def placed(pieces, t, axis):
    return jnp.concatenate(unxor(pieces, t), axis=axis)


def reduce4(pieces):
    far = (pieces[2].astype(F32) + px(pieces[3], 1).astype(F32)).astype(BF)
    return pieces[0], px(pieces[1], 1), px(far, 2)


def halved(blocks, s, early=None):
    for axis, bits, place in ((1, 2, 1), (1, 1, 0), (0, 4, 2)):
        mine = (s >> place) & 1
        keep = lax.dynamic_index_in_dim(blocks, mine, axis, keepdims=False)
        send = lax.dynamic_index_in_dim(blocks, 1 - mine, axis, keepdims=False)
        got = ps(send.astype(BF), bits)
        if bits == 4 and early:
            got, *early[:] = after(got, *early)
        blocks = keep.astype(F32) + got.astype(F32)
    return blocks


def spans_of(image_ids, row_count, first_row, margin, near):
    tokens = image_ids.shape[0]
    most = tokens // IMG_LEAST + 1
    place = jnp.arange(tokens, dtype=jnp.int32)
    names = jnp.arange(most, dtype=jnp.int32)[:, None]
    same = image_ids[None, :] == names
    low = jnp.min(jnp.where(same, place[None, :], tokens), axis=1)
    high = jnp.max(jnp.where(same, place[None, :] + 1, 0), axis=1)
    own = lax.dynamic_slice_in_dim(image_ids, first_row, row_count, 0)
    mine = own[None, :] == names
    start = jnp.sum(jnp.where(mine, low[:, None], 0), axis=0)
    end = jnp.sum(jnp.where(mine, high[:, None], 0), axis=0)
    valid = own >= 0
    shift = margin - first_row
    start = jnp.where(valid, start + shift, 0)
    end = jnp.where(valid, end + shift, 0)
    lo = jnp.min(jnp.where(valid, start, near).reshape(-1, TILE), axis=1)
    hi = jnp.max(end.reshape(-1, TILE), axis=1)
    lo = jnp.clip(lo // TILE, 0, near // TILE)
    hi = jnp.clip(-(-hi // TILE), 0, near // TILE)
    spans = jnp.concatenate(
        [start[None, :], end[None, :], jnp.zeros((6, row_count), jnp.int32)], axis=0
    )
    return spans, jnp.stack([lo, hi], axis=1).reshape(-1)


def per_device(
    block_input,
    cotangent,
    image_ids,
    qkv_weight,
    proj_weight,
    fc1_weight,
    fc2_weight,
    norm1_gain,
    norm1_shift,
    q_bias,
    v_bias,
    proj_bias,
    scale_attn,
    norm2_gain,
    norm2_shift,
    fc1_bias,
    fc2_bias,
    scale_mlp,
):
    row_count, fw = block_input.shape
    n_seq = lax.axis_size("seq")
    width = 4 * fw
    features = qkv_weight.shape[0]
    sub = row_count // 4
    t = lax.axis_index("tensor").astype(jnp.int32)
    s = lax.axis_index("seq").astype(jnp.int32)
    reach = (IMG - 1 + row_count - 1) // row_count
    tile_rows = min(128, row_count)

    xs = gather4(block_input)
    if n_seq == 8:
        own = jnp.concatenate([qkv_weight, proj_weight], axis=1)
        z2, z4, z6 = ps(own, 2), ps(own, 4), ps(own, 6)
        found = [None] * 8
        for bits, piece in ((0, own), (2, z2), (4, z4), (6, z6)):
            found[bits] = piece
            found[bits ^ 1] = ps(piece, 1)
        w_qkv = jnp.zeros((8,) + own.shape, BF)
        for bits in range(8):
            w_qkv = lax.dynamic_update_slice(w_qkv, found[bits][None], (s ^ bits, 0, 0))
    else:
        w_qkv = jnp.concatenate(
            [
                lax.all_gather(w, "seq", axis=1, tiled=True)[None]
                for w in (qkv_weight, proj_weight)
            ],
            axis=2,
        )
    vec_own = jnp.stack(
        [
            norm1_gain,
            norm1_shift,
            norm2_gain,
            norm2_shift,
            proj_bias,
            scale_attn,
            fc2_bias,
            scale_mlp,
        ]
    )
    vec = placed([vec_own] + [px(vec_own, r) for r in range(1, 4)], t, 1)
    units = fc1_weight.shape[0]

    offsets_of = []
    counts = []
    for place in range(2 * reach + 1):
        offset = reach - place
        if offset == 0:
            count = row_count
        else:
            need = IMG - 1 - (abs(offset) - 1) * row_count
            count = min(row_count, -(-need // tile_rows) * tile_rows)
        offsets_of.append(offset)
        counts.append(count)
    offsets = [sum(counts[:k]) for k in range(len(counts))]
    near = sum(counts)
    margin = offsets[reach]
    spans, edges = spans_of(image_ids, row_count, s * row_count, margin, near)
    sc = jnp.concatenate([t[None], edges])
    sc_t = t[None]

    normed1, query, kv0, kv1, w_full, proj_full = qkv_call(
        sc_t, xs, w_qkv, vec, q_bias[None, :], v_bias[None, :]
    )
    nears = []
    for kv in (kv0, kv1):
        pieces = []
        for offset, count in zip(offsets_of, counts):
            if offset == 0:
                pieces.append(kv)
            elif offset > 0:
                pieces.append(passed_along(kv[row_count - count :], offset))
            else:
                pieces.append(passed_along(kv[:count], offset))
        nears.append(pieces)
    cots = swap4([rows_at(cotangent, t ^ r, sub) for r in range(4)])
    grad_second = (
        jnp.concatenate(unxor(cots, t), axis=1).astype(F32) * vec[7:8, :]
    ).astype(BF)
    grads = gather4(grad_second)
    contexts = []
    stats = []
    stacked = jnp.concatenate([fc1_weight, fc2_weight], axis=0)
    stacked, *nears[0] = after(stacked, *nears[0])
    others = lax.all_gather(stacked, "seq", axis=1, tiled=True)
    ws = gather4(proj_full)
    for pair in range(2):
        ctx, st = fwd_call(pair, sc, query, spans, nears[pair], offsets, counts)
        if pair == 0:
            ctx, *rest = after(ctx, *ws, *grads)
            ws, grads = rest[:4], rest[4:]
        contexts.append(ctx)
        stats.append(st)
    context = jnp.concatenate(contexts, axis=1)
    ctx_rows = swap4([rows_at(context, t ^ r, sub) for r in range(4)])
    branch, middle, normed2 = proj_call(sc_t, ctx_rows, ws, xs, vec)
    n_near = px(normed2, 1)
    n_across = px(normed2, 2)
    n_far = px(n_across, 1)
    bias1 = fc1_bias[None, :]
    hid_b, gb_b, s2, s3, d2, d3, fb_b = mlp_call((n_across, n_far), grads[2:], others, bias1)
    far = (d2.astype(F32) + px(d3, 1).astype(F32)).astype(BF)
    far, n_near = after(far, n_near)
    far = px(far, 2)
    hid_a, gb_a, s0, s1, d0, d1, fb_a = mlp_call((normed2, n_near), grads[:2], others, bias1)
    from_near = px(d1, 1)

    fc_part = wgrad_call((normed2, n_near, n_across, n_far), grads, (gb_a, gb_b), (hid_a, hid_b))
    far, fc_part = after(far, fc_part)
    fc_out = lax.psum_scatter(fc_part, "seq", scatter_dimension=0, tiled=True)
    grad_middle, grad_branch, grad_ctx, sums_mid = mid_call(
        sc_t, (d0, from_near, far), cots, middle, branch, ws, vec
    )
    grad_rows = jnp.stack(swap4([grad_ctx[r] for r in range(4)]))
    grad_rows, grad_branch, s0, s1, s2, s3 = after(grad_rows, grad_branch, s0, s1, s2, s3)
    seconds = reduce4([s0, s1, s2, s3])
    branch_all = gather4(grad_branch)

    grad_q = []
    grad_k = []
    grad_v = []
    for pair in range(2):
        got = bwd_call(
            pair, sc, query, spans, stats[pair], grad_rows, nears[pair], offsets, counts, reach
        )
        got = list(got)
        if pair == 0:
            got[1], grad_rows = after(got[1], grad_rows)
        if pair == 0:
            got[0], *branch_all = after(got[0], *branch_all)
            branch_rows = placed(branch_all, t, 0)
            proj_part = tn(branch_rows, context).astype(BF)
            if n_seq == 8:
                proj_out = halved(proj_part.reshape(2, 2, 2, width // 8, features), s)
            else:
                proj_out = lax.psum_scatter(proj_part, "seq", scatter_dimension=0, tiled=True)
        else:
            got[0], *seconds = after(got[0], *seconds)
            o0, o1, o2, o3, sums_out = out_call(sc_t, seconds, cots, middle, vec)
            block_output = placed(swap4([o0, o1, o2, o3]), t, 0)
        grad_q.append(got[0])
        backs = [
            passed_along(got[1 + k], -offset)
            for k, offset in enumerate(offsets_of)
            if offset != 0
        ]
        if pair == 1:
            *backs, block_output = after(*backs, block_output)
        total = got[1 + reach]
        others_of = [(o, c) for o, c in zip(offsets_of, counts) if o != 0]
        for back, (offset, count) in zip(backs, others_of):
            back = back.astype(F32)
            if count < row_count:
                gap = row_count - count
                ends = ((gap, 0), (0, 0)) if offset > 0 else ((0, gap), (0, 0))
                back = jnp.pad(back, ends)
            total = total + back
        total = total.astype(BF)
        grad_k.append(total[:, :PAIR])
        grad_v.append(total[:, PAIR:])
    gk = jnp.concatenate(grad_k, axis=1)
    gv = jnp.concatenate(grad_v, axis=1)
    gq = jnp.concatenate(grad_q, axis=1)
    finals = [
        proj_out.T.astype(F32),
        fc_out[:, :units].T.astype(F32),
        fc_out[:, units:].T.astype(F32),
    ]
    if n_seq == 8:
        unit = width // 8
        blocks = qkvg_call(gq, gk, gv, normed1).reshape(2, 2, 2, 3, features, unit)
        blocks, gk = after(blocks, gk)
        blocks = halved(blocks, s, finals)
        qkv_out = jnp.concatenate([blocks[k] for k in range(3)], axis=1)
    else:
        qkv_parts = [tn(g, normed1) for g in (gq, gk, gv)]
        qkv_out = lax.psum_scatter(
            jnp.stack(qkv_parts, axis=1).reshape(features, 3 * width).astype(BF),
            "seq",
            scatter_dimension=1,
            tiled=True,
        ).astype(F32)
    pieces = gn1_call(sc_t, grad_q[0], grad_q[1], gk, gv, w_full)
    sums_last = nsum_call(sc_t, pieces, xs)
    i0, i1, i2, i3 = last_call(sc_t, reduce4(pieces), xs, grad_middle, vec)
    rows8 = jnp.concatenate([sums_last[0:2], sums_mid[0:4], sums_out[0:2]], axis=0)
    cut = [lax.dynamic_slice_in_dim(rows8, (t ^ r) * fw, fw, 1) for r in range(4)]
    got = swap4(cut)
    own8 = got[0] + got[1] + got[2] + got[3]
    flat = jnp.concatenate(
        [
            own8.reshape(-1),
            jnp.sum(gq.astype(F32), axis=0),
            jnp.sum(gv.astype(F32), axis=0),
            fb_a[0] + fb_b[0],
        ]
    ).reshape(-1, 128)
    flat, i0, i1, i2, i3 = after(flat, i0, i1, i2, i3)
    input_grad = placed(swap4([i0, i1, i2, i3]), t, 0)
    if n_seq == 8:
        for bits in (2, 1, 4):
            flat = flat + ps(flat, bits)
    else:
        flat = lax.psum(flat, "seq")
    flat = flat.reshape(-1)
    own8 = flat[: 8 * fw].reshape(8, fw)
    q_bias_grad = flat[8 * fw : 8 * fw + features]
    v_bias_grad = flat[8 * fw + features : 8 * fw + 2 * features]
    fc1_bias_grad = flat[8 * fw + 2 * features :]
    return (
        block_output,
        input_grad,
        qkv_out,
        *finals,
        own8[0],
        own8[1],
        q_bias_grad,
        v_bias_grad,
        own8[5],
        own8[4],
        own8[2],
        own8[3],
        fc1_bias_grad,
        own8[7],
        own8[6],
    )


def solution(mesh):
    cut = P("tensor", "seq")
    by_tensor = P("tensor")
    in_specs = (P("seq", "tensor"), P("seq", "tensor"), P()) + (cut,) * 4 + (by_tensor,) * 11
    out_specs = (P("seq", "tensor"), P("seq", "tensor")) + (cut,) * 4 + (by_tensor,) * 11

    return jax.shard_map(
        per_device, mesh=mesh, in_specs=in_specs, out_specs=out_specs, check_vma=False
    )
```
